256 devices in a mesh: tm: 32 (over x, y, core), space: 8 (over z).
Axes of the slice: x: 4, y: 4, z: 8, core: 2. Of those that a mesh axis runs over, the one named last changes fastest.
Arguments:
- snapshots: bfloat16 [512, 524288], P('tm', 'space'), may hold values from -6 to 6
- block_lists: int32 [8192, 2], P(('tm', 'space')), may hold values from 0 to 8191
- tile_counts: int32 [8192], P(('tm', 'space')), may hold values from 1 to 2
- remap_weights: bfloat16 [8192, 64, 128], P(('tm', 'space')), may hold values from -0.5 to 0.5
- basis: bfloat16 [524288, 1024], P(('tm', 'space')), may hold values from -6 to 6
- variances: float32 [1024], replicated, may hold values from 0.3 to 3
Outputs:
- coeffs: float32 [1024, 512], P('space')
- rotated: bfloat16 [524288, 1024], P(('tm', 'space'))
The draws below stay inside these ranges and needn't reach their ends.
Inputs may be any that keep to these rules, and one draw needn't show every extreme that they name: `block_lists`: slots at or beyond a tile's count carry no weight.
All inputs are finite; a program needn't handle non-finite values.
Results may differ from the reference program's by a relative error of at most 0.0043.
Values may be sent and summed in bfloat16 or wider, within the bound.
No kernel may reach another device: no remote copies, remote signals or barrier semaphores. Data moves between devices by JAX's collectives and lax.ppermute only.
A program may use at most 192 MiB of HBM per device.

```python
import math
import jax
import jax.numpy as jnp
from jax import lax

K = 1024
TILE = 64
MAXB = 2
TILES_DEV = 32
NT = 8192
NP = 524288
T_SIZE = 512


def with_ends(array, key, low, high):
    index_at = [jax.random.randint(jax.random.fold_in(key, axis), (), 0, length) for axis, length in enumerate(array.shape)]
    longest = array.shape.index(max(array.shape))
    neighbour = index_at[:longest] + [(index_at[longest] + 1) % array.shape[longest]] + index_at[longest + 1:]
    return array.at[tuple(index_at)].set(low).at[tuple(neighbour)].set(high)


def block_levels(stream_key, shape, shards, smallest, top_value):
    def one(dim, shards_of):
        draws = jax.random.uniform(jax.random.fold_in(jax.random.fold_in(stream_key, 6), dim), (shards_of,), jnp.float32, smallest / len(shards), top_value / len(shards))
        return jnp.repeat(jnp.exp(draws), shape[dim] // shards_of).reshape((-1,) + (1,) * (len(shape) - dim - 1))

    loudness = one(*shards[0])
    for cut in shards[1:]:
        loudness = loudness * one(*cut)
    return loudness


def centred(key, shape, spread, bound, shards=(), kind=jnp.bfloat16):
    array = spread * jax.random.normal(key, shape, jnp.float32)
    if shards:
        array = array * block_levels(key, shape, shards, -0.22, 0.18)
    return jnp.clip(array, -bound, bound).astype(kind)


def setup_inputs(seed: int = 0) -> dict:
    splits = jax.random.split(jax.random.key(seed), 7)
    return {
        "snapshots": centred(splits[0], (T_SIZE, NP), 1.0, 6.0, ((0, 32), (1, 8))),
        "block_lists": with_ends(jax.random.randint(splits[1], (NT, MAXB), 0, NT), jax.random.fold_in(splits[1], 1), 0, NT - 1).astype(jnp.int32),
        "tile_counts": with_ends(jax.random.randint(splits[2], (NT,), 1, MAXB + 1), jax.random.fold_in(splits[2], 1), 1, MAXB).astype(jnp.int32),
        "remap_weights": centred(splits[3], (NT, TILE, MAXB * TILE), (MAXB * TILE) ** -0.5, 0.5, ((0, 256),)),
        "basis": centred(splits[4], (NP, K), 1.0, 6.0, ((0, 256),)),
        "variances": jnp.clip(jnp.exp(jax.random.uniform(splits[5], (K,), jnp.float32, math.log(0.3), math.log(3.0))), 0.3, 3.0),
    }


def reference(snapshots, block_lists, tile_counts, remap_weights, basis, variances):
    sources = snapshots.reshape(T_SIZE, NT, TILE)
    slot_index = jnp.arange(MAXB * TILE, dtype=jnp.int32) // TILE

    def remap_block(packed):
        block_ids, slot_counts, weights = packed
        picked = sources[:, block_ids.reshape(-1), :].reshape(T_SIZE, block_ids.shape[0], MAXB * TILE)
        keep = slot_index[None, :] < slot_counts[:, None]
        masked = jnp.where(keep[:, None, :], weights, jnp.zeros_like(weights))
        result = jnp.einsum('kip,tkp->kit', masked.astype(jnp.float32), picked.astype(jnp.float32))
        return result.astype(jnp.bfloat16)
    group_count = NT // TILES_DEV
    blocked = lax.map(remap_block, (block_lists.reshape(group_count, TILES_DEV, MAXB), tile_counts.reshape(group_count, TILES_DEV), remap_weights.reshape(group_count, TILES_DEV, TILE, MAXB * TILE)))
    remapped = blocked.reshape(NP, T_SIZE)
    coeffs = lax.dot_general(basis, remapped, (((0,), (0,)), ((), ())), preferred_element_type=jnp.float32) / math.sqrt(NP)
    coeff_half = coeffs.astype(jnp.bfloat16)
    update = lax.dot_general(remapped, coeff_half, (((1,), (1,)), ((), ())), preferred_element_type=jnp.float32) / math.sqrt(T_SIZE)
    rotated = (basis.astype(jnp.float32) * variances[None, :] + update).astype(jnp.bfloat16)
    return (coeffs, rotated)
```

```python
import functools
import math

import jax
import jax.numpy as jnp
from jax import lax
from jax.experimental import pallas as pl
from jax.experimental.pallas import tpu as pltpu
from jax.sharding import PartitionSpec as P

TILE = 64
MAXB = 2
PAIR = MAXB * TILE
ROWS = 8
BF16 = jnp.bfloat16
F32 = jnp.float32


def pick_kernel(tiles, per_space, sel_ref, source_ref, out_ref):
    group = pl.program_id(0) * out_ref.shape[0]
    low = lax.broadcasted_iota(jnp.int32, (ROWS, PAIR), 1) < TILE

    def fetch(slot):
        block = sel_ref[slot]
        within = lax.rem(block, per_space)
        lanes = pl.ds(pl.multiple_of(lax.div(within, 2) * PAIR, PAIR), PAIR)
        found = source_ref[lax.div(block, per_space), :, lanes]
        swapped = jnp.concatenate([found[:, TILE:], found[:, :TILE]], axis=1)
        return found, swapped, lax.rem(within, 2) == 1

    for owner in range(out_ref.shape[0]):
        def tile(k, carry):
            slot = ((group + owner) * tiles + k) * MAXB
            a, a_swapped, a_odd = fetch(slot)
            b, b_swapped, b_odd = fetch(slot + 1)
            first = jnp.where(a_odd, a_swapped, a)
            second = jnp.where(b_odd, b, b_swapped)
            lanes = pl.ds(pl.multiple_of(k * PAIR, PAIR), PAIR)
            out_ref[owner, :, lanes] = jnp.where(low, first, second)
            return carry

        lax.fori_loop(0, tiles, tile, 0, unroll=8)


def pick(sel, source, owners, tiles, interpret=False):
    spaces, rows, cells = source.shape
    step = min(8, owners)
    return pl.pallas_call(
        functools.partial(pick_kernel, tiles, cells // TILE),
        out_shape=jax.ShapeDtypeStruct((owners, rows, tiles * PAIR), BF16),
        grid_spec=pltpu.PrefetchScalarGridSpec(
            num_scalar_prefetch=1,
            grid=(owners // step,),
            in_specs=[
                pl.BlockSpec((spaces, rows, cells), lambda i, sel: (0, 0, 0), pipeline_mode=pl.Buffered(1)),
            ],
            out_specs=pl.BlockSpec((step, rows, tiles * PAIR), lambda i, sel: (i, 0, 0)),
        ),
        compiler_params=pltpu.CompilerParams(vmem_limit_bytes=40 << 20),
        name="pick",
        interpret=interpret,
    )(sel, source)


def project_kernel(group, counts_ref, picked_ref, weights_ref, basis_ref, remapped_ref, partial_ref):
    step = pl.program_id(0)

    @pl.when(step == 0)
    def _():
        partial_ref[...] = jnp.zeros_like(partial_ref)

    low = lax.broadcasted_iota(jnp.int32, (TILE, PAIR), 1) < TILE
    pieces = []
    for k in range(group):
        both = counts_ref[step * group + k] > 1
        weights = jnp.where(jnp.logical_or(low, both), weights_ref[k].astype(F32), 0.0).astype(BF16)
        picked = picked_ref[:, k * PAIR:(k + 1) * PAIR]
        pieces.append(
            lax.dot_general(weights, picked, (((1,), (1,)), ((), ())), preferred_element_type=F32)
        )
    block = jnp.concatenate(pieces, axis=0).astype(BF16)
    remapped_ref[...] = block
    partial_ref[...] += jnp.dot(block.T, basis_ref[...], preferred_element_type=F32)


def project(counts, picked, weights, basis, interpret=False):
    snaps = picked.shape[0]
    tiles = weights.shape[0]
    cells, rank = basis.shape
    group = 4
    return pl.pallas_call(
        functools.partial(project_kernel, group),
        out_shape=(
            jax.ShapeDtypeStruct((cells, snaps), BF16),
            jax.ShapeDtypeStruct((snaps, rank), F32),
        ),
        grid_spec=pltpu.PrefetchScalarGridSpec(
            num_scalar_prefetch=1,
            grid=(tiles // group,),
            in_specs=[
                pl.BlockSpec((snaps, group * PAIR), lambda i, counts: (0, i)),
                pl.BlockSpec((group, TILE, PAIR), lambda i, counts: (i, 0, 0)),
                pl.BlockSpec((group * TILE, rank), lambda i, counts: (i, 0)),
            ],
            out_specs=(
                pl.BlockSpec((group * TILE, snaps), lambda i, counts: (i, 0)),
                pl.BlockSpec((snaps, rank), lambda i, counts: (0, 0)),
            ),
        ),
        compiler_params=pltpu.CompilerParams(vmem_limit_bytes=40 << 20),
        name="project",
        interpret=interpret,
    )(counts, picked, weights, basis)


def rotate_kernel(scale, r0_ref, r1_ref, c0_ref, c1_ref, basis_ref, variances_ref, out_ref):
    update = jnp.dot(r0_ref[...], c0_ref[...], preferred_element_type=F32)
    update += jnp.dot(r1_ref[...], c1_ref[...], preferred_element_type=F32)
    out_ref[...] = (basis_ref[...].astype(F32) * variances_ref[...] + update * scale).astype(BF16)


def rotate(remapped, halves, basis, variances, interpret=False):
    cells, rank = basis.shape
    snaps = remapped[0].shape[1]
    rows = min(256, cells)
    resident = lambda i: (0, 0)
    return pl.pallas_call(
        functools.partial(rotate_kernel, 1.0 / math.sqrt(2 * snaps)),
        out_shape=jax.ShapeDtypeStruct((cells, rank), BF16),
        grid=(cells // rows,),
        in_specs=[
            pl.BlockSpec((rows, snaps), lambda i: (i, 0)),
            pl.BlockSpec((rows, snaps), lambda i: (i, 0)),
            pl.BlockSpec((snaps, rank), resident),
            pl.BlockSpec((snaps, rank), resident),
            pl.BlockSpec((rows, rank), lambda i: (i, 0)),
            pl.BlockSpec((1, rank), resident),
        ],
        out_specs=pl.BlockSpec((rows, rank), lambda i: (i, 0)),
        compiler_params=pltpu.CompilerParams(vmem_limit_bytes=40 << 20),
        name="rotate",
        interpret=interpret,
    )(*remapped, *halves, basis, variances[None, :])


def exchange(array, axis):
    return lax.all_to_all(array, axis, split_axis=0, concat_axis=0, tiled=True)


def per_device(interpret, snapshots, block_lists, tile_counts, remap_weights, basis, variances):
    tiles = block_lists.shape[0]
    owners, spaces = lax.axis_size("tm"), lax.axis_size("space")
    cells, rank = basis.shape
    total = cells * owners * spaces
    own_ranks = rank // spaces
    here = lax.axis_index("space")

    sources = [
        lax.all_gather(snapshots[c * ROWS:(c + 1) * ROWS], "space", axis=0) for c in range(2)
    ]
    sel = lax.all_gather(block_lists, "tm", axis=0, tiled=True).reshape(-1)

    remapped, messages = [], []
    for source in sources:
        if messages:
            source, messages[0] = lax.optimization_barrier((source, messages[0]))
        picked = pick(sel, source, owners, tiles, interpret)
        arrived = exchange(picked, "tm").reshape(owners * ROWS, tiles * PAIR)
        block, partial = project(tile_counts, arrived, remap_weights, basis, interpret)
        parts = exchange(partial.reshape(owners, ROWS, rank), "tm")
        column = jnp.sum(parts, axis=0)
        column = exchange(jnp.broadcast_to(column, (spaces, ROWS, rank)), "space")
        coeffs = jnp.sum(column, axis=0) * (1.0 / math.sqrt(total))
        half = coeffs.astype(BF16)
        rest = lax.dynamic_slice_in_dim(coeffs - half.astype(F32), here * own_ranks, own_ranks, 1)
        messages.append(jnp.concatenate([half, rest.astype(BF16)], axis=1))
        remapped.append(block)

    message = jnp.concatenate(messages, axis=0)
    everyone = exchange(jnp.broadcast_to(message, (owners,) + message.shape), "tm")
    halves = [
        everyone[:, c * ROWS:(c + 1) * ROWS, :rank].reshape(owners * ROWS, rank) for c in range(2)
    ]
    high = lax.dynamic_slice_in_dim(everyone, here * own_ranks, own_ranks, 2)
    own = high.astype(F32) + everyone[:, :, rank:].astype(F32)
    own_coeffs = own.reshape(owners * 2 * ROWS, own_ranks).T
    rotated = rotate(remapped, halves, basis, variances, interpret)
    return (own_coeffs, rotated)


def solution(mesh, interpret=False):
    return jax.shard_map(
        functools.partial(per_device, interpret),
        mesh=mesh,
        in_specs=(
            P("tm", "space"),
            P(("tm", "space"), None),
            P(("tm", "space")),
            P(("tm", "space"), None, None),
            P(("tm", "space"), None),
            P(),
        ),
        out_specs=(P("space", None), P(("tm", "space"), None)),
        check_vma=False,
    )
```

```python
import functools
import math

import jax
import jax.numpy as jnp
from jax import lax
from jax.experimental import pallas as pl
from jax.experimental.pallas import tpu as pltpu
from jax.sharding import PartitionSpec as P

TILE = 64
MAXB = 2
PAIR = MAXB * TILE
ROWS = 8
BF16 = jnp.bfloat16
F32 = jnp.float32


def pick_kernel(sel_ref, source_ref, out_ref):
    count = out_ref.shape[0]
    start = pl.program_id(0) * count
    low = lax.broadcasted_iota(jnp.int32, (ROWS, PAIR), 1) < TILE

    def fetch(slot):
        block = sel_ref[slot]
        found = source_ref[lax.shift_right_logical(block, 1)]
        swapped = jnp.concatenate([found[:, TILE:], found[:, :TILE]], axis=1)
        return found, swapped, (block & 1) == 1

    def tile(k, carry):
        slot = (start + k) * MAXB
        a, a_swapped, a_odd = fetch(slot)
        b, b_swapped, b_odd = fetch(slot + 1)
        first = jnp.where(a_odd, a_swapped, a)
        second = jnp.where(b_odd, b, b_swapped)
        out_ref[k] = jnp.where(low, first, second)
        return carry

    lax.fori_loop(0, count, tile, 0, unroll=8)


def pick(sel, source, interpret=False):
    count = sel.shape[0] // MAXB
    step = min(128, count)
    return pl.pallas_call(
        pick_kernel,
        out_shape=jax.ShapeDtypeStruct((count, ROWS, PAIR), BF16),
        grid_spec=pltpu.PrefetchScalarGridSpec(
            num_scalar_prefetch=1,
            grid=(count // step,),
            in_specs=[
                pl.BlockSpec(source.shape, lambda i, sel: (0, 0, 0), pipeline_mode=pl.Buffered(1)),
            ],
            out_specs=pl.BlockSpec((step, ROWS, PAIR), lambda i, sel: (i, 0, 0)),
        ),
        compiler_params=pltpu.CompilerParams(vmem_limit_bytes=40 << 20),
        name="pick",
        interpret=interpret,
    )(sel, source)


def project_kernel(group, counts_ref, picked_ref, weights_ref, basis_ref, remapped_ref, partial_ref):
    step = pl.program_id(0)

    @pl.when(step == 0)
    def _():
        partial_ref[...] = jnp.zeros_like(partial_ref)

    low = lax.broadcasted_iota(jnp.int32, (TILE, PAIR), 1) < TILE
    pieces = []
    for k in range(group):
        both = counts_ref[step * group + k] > 1
        weights = jnp.where(jnp.logical_or(low, both), weights_ref[k].astype(F32), 0.0).astype(BF16)
        picked = picked_ref[:, k].reshape(-1, PAIR)
        pieces.append(
            lax.dot_general(weights, picked, (((1,), (1,)), ((), ())), preferred_element_type=F32)
        )
    block = jnp.concatenate(pieces, axis=0).astype(BF16)
    remapped_ref[...] = block
    partial_ref[...] += jnp.dot(block.T, basis_ref[...], preferred_element_type=F32)


def project(counts, picked, weights, basis, interpret=False):
    snaps = picked.shape[0] * ROWS
    tiles = weights.shape[0]
    cells, rank = basis.shape
    group = 4
    return pl.pallas_call(
        functools.partial(project_kernel, group),
        out_shape=(
            jax.ShapeDtypeStruct((cells, snaps), BF16),
            jax.ShapeDtypeStruct((snaps, rank), F32),
        ),
        grid_spec=pltpu.PrefetchScalarGridSpec(
            num_scalar_prefetch=1,
            grid=(tiles // group,),
            in_specs=[
                pl.BlockSpec((picked.shape[0], group, ROWS, PAIR), lambda i, counts: (0, i, 0, 0)),
                pl.BlockSpec((group, TILE, PAIR), lambda i, counts: (i, 0, 0)),
                pl.BlockSpec((group * TILE, rank), lambda i, counts: (i, 0)),
            ],
            out_specs=(
                pl.BlockSpec((group * TILE, snaps), lambda i, counts: (i, 0)),
                pl.BlockSpec((snaps, rank), lambda i, counts: (0, 0)),
            ),
        ),
        compiler_params=pltpu.CompilerParams(vmem_limit_bytes=40 << 20),
        name="project",
        interpret=interpret,
    )(counts, picked, weights, basis)


def rotate_kernel(scale, r0_ref, r1_ref, c0_ref, c1_ref, basis_ref, variances_ref, out_ref):
    update = jnp.dot(r0_ref[...], c0_ref[...], preferred_element_type=F32)
    update += jnp.dot(r1_ref[...], c1_ref[...], preferred_element_type=F32)
    out_ref[...] = (basis_ref[...].astype(F32) * variances_ref[...] + update * scale).astype(BF16)


def rotate(remapped, halves, basis, variances, interpret=False):
    cells, rank = basis.shape
    snaps = remapped[0].shape[1]
    rows = min(256, cells)
    resident = lambda i: (0, 0)
    return pl.pallas_call(
        functools.partial(rotate_kernel, 1.0 / math.sqrt(2 * snaps)),
        out_shape=jax.ShapeDtypeStruct((cells, rank), BF16),
        grid=(cells // rows,),
        in_specs=[
            pl.BlockSpec((rows, snaps), lambda i: (i, 0)),
            pl.BlockSpec((rows, snaps), lambda i: (i, 0)),
            pl.BlockSpec((snaps, rank), resident),
            pl.BlockSpec((snaps, rank), resident),
            pl.BlockSpec((rows, rank), lambda i: (i, 0)),
            pl.BlockSpec((1, rank), resident),
        ],
        out_specs=pl.BlockSpec((rows, rank), lambda i: (i, 0)),
        compiler_params=pltpu.CompilerParams(vmem_limit_bytes=40 << 20),
        name="rotate",
        interpret=interpret,
    )(*remapped, *halves, basis, variances[None, :])


def exchange(array, axis):
    return lax.all_to_all(array, axis, split_axis=0, concat_axis=0, tiled=True)


def per_device(interpret, snapshots, block_lists, tile_counts, remap_weights, basis, variances):
    tiles = block_lists.shape[0]
    owners, spaces = lax.axis_size("tm"), lax.axis_size("space")
    cells, rank = basis.shape
    total = cells * owners * spaces
    own_ranks = rank // spaces
    here = lax.axis_index("space")

    sources = [
        lax.all_gather(snapshots[c * ROWS:(c + 1) * ROWS], "space", axis=0) for c in range(2)
    ]
    sel = lax.all_gather(block_lists, "tm", axis=0, tiled=True).reshape(-1)

    remapped, messages = [], []
    for source in sources:
        if messages:
            source, messages[0] = lax.optimization_barrier((source, messages[0]))
        source = source.reshape(spaces, ROWS, -1, PAIR).transpose(0, 2, 1, 3)
        picked = pick(sel, source.reshape(-1, ROWS, PAIR), interpret)
        arrived = exchange(picked.reshape(owners, tiles, ROWS, PAIR), "tm")
        block, partial = project(tile_counts, arrived, remap_weights, basis, interpret)
        parts = exchange(partial.reshape(owners, ROWS, rank), "tm")
        column = jnp.sum(parts, axis=0)
        column = exchange(jnp.broadcast_to(column, (spaces, ROWS, rank)), "space")
        coeffs = jnp.sum(column, axis=0) * (1.0 / math.sqrt(total))
        half = coeffs.astype(BF16)
        rest = lax.dynamic_slice_in_dim(coeffs - half.astype(F32), here * own_ranks, own_ranks, 1)
        messages.append(jnp.concatenate([half, rest.astype(BF16)], axis=1))
        remapped.append(block)

    message = jnp.concatenate(messages, axis=0)
    everyone = exchange(jnp.broadcast_to(message, (owners,) + message.shape), "tm")
    halves = [
        everyone[:, c * ROWS:(c + 1) * ROWS, :rank].reshape(owners * ROWS, rank) for c in range(2)
    ]
    high = lax.dynamic_slice_in_dim(everyone, here * own_ranks, own_ranks, 2)
    own = high.astype(F32) + everyone[:, :, rank:].astype(F32)
    own_coeffs = own.reshape(owners * 2 * ROWS, own_ranks).T
    rotated = rotate(remapped, halves, basis, variances, interpret)
    return (own_coeffs, rotated)


def solution(mesh, interpret=False):
    return jax.shard_map(
        functools.partial(per_device, interpret),
        mesh=mesh,
        in_specs=(
            P("tm", "space"),
            P(("tm", "space"), None),
            P(("tm", "space")),
            P(("tm", "space"), None, None),
            P(("tm", "space"), None),
            P(),
        ),
        out_specs=(P("space", None), P(("tm", "space"), None)),
        check_vma=False,
    )
```

```python
import functools
import math

import jax
import jax.numpy as jnp
from jax import lax
from jax.experimental import pallas as pl
from jax.experimental.pallas import tpu as pltpu
from jax.sharding import PartitionSpec as P


TILE = 64
MAXB = 2
PAIR = MAXB * TILE
ROWS = 8
LANES = 128
CAPACITY = 256
BF16 = jnp.bfloat16
F32 = jnp.float32


def pair_words(index):
    after = pltpu.roll(index, LANES - 1, 1)
    return (
        lax.shift_right_logical(index, 1)
        | (lax.shift_right_logical(after, 1) << 12)
        | ((index & 1) << 24)
        | ((1 - (after & 1)) << 25)
    )


def route_kernel(capacity, per_space, here_ref, codes_ref, request_ref, local_ref):
    owners = codes_ref.shape[0]
    spaces = request_ref.shape[0]
    here = here_ref[0]
    codes = codes_ref[...]
    owner_of = jnp.where(codes < 0, -1, lax.div(jnp.maximum(codes, 0), per_space))
    within = jnp.where(codes < 0, 0, lax.rem(jnp.maximum(codes, 0), per_space))
    upper = lax.broadcasted_iota(jnp.int32, (LANES, LANES), 0) <= lax.broadcasted_iota(jnp.int32, (LANES, LANES), 1)
    upper = jnp.where(upper, 1.0, 0.0).astype(BF16)
    lower = lax.broadcasted_iota(jnp.int32, (owners, owners), 0) > lax.broadcasted_iota(jnp.int32, (owners, owners), 1)
    lower = jnp.where(lower, 1.0, 0.0).astype(BF16)
    location = jnp.zeros_like(codes)
    target = jnp.full_like(codes, -1)
    most = jnp.zeros((1, LANES), F32)
    for s in range(spaces):
        match = owner_of == s
        ones = jnp.where(match, 1.0, 0.0).astype(BF16)
        prefix = jnp.dot(ones, upper, preferred_element_type=F32)
        sums = jnp.broadcast_to(prefix[:, LANES - 1:], (owners, LANES))
        ahead = jnp.dot(lower, sums.astype(BF16), preferred_element_type=F32)
        rank = (prefix + ahead).astype(jnp.int32) - 1
        most = jnp.maximum(most, ahead[owners - 1:] + sums[owners - 1:])
        location = jnp.where(match, rank + lax.rem(here - s + spaces, spaces) * capacity, location)
        target = jnp.where(match, rank + s * capacity, target)
    local_ref[...] = pair_words(location)

    rows = spaces * capacity // LANES
    row_id = lax.broadcasted_iota(jnp.int32, (rows, LANES), 0)
    lane_id = lax.broadcasted_iota(jnp.int32, (LANES, LANES), 1)
    lane_of = (target & (LANES - 1)).astype(F32)
    lane_of = jnp.concatenate([lane_of, jnp.zeros((LANES - owners, LANES), F32)], axis=0).T
    high = jnp.zeros((rows, LANES), F32)
    low = jnp.zeros((rows, LANES), F32)
    for r in range(owners):
        hit = jnp.broadcast_to(target[r:r + 1] >> 7, (rows, LANES)) == row_id
        value = jnp.broadcast_to(within[r:r + 1], (rows, LANES))
        upper_part = jnp.where(hit, lax.shift_right_logical(value, 6), 0).astype(F32).astype(BF16)
        lower_part = jnp.where(hit, value & 63, 0).astype(F32).astype(BF16)
        column = jnp.broadcast_to(lane_of[:, r:r + 1], (LANES, LANES)).astype(jnp.int32)
        onehot = jnp.where(column == lane_id, 1.0, 0.0).astype(BF16)
        high += jnp.dot(upper_part, onehot, preferred_element_type=F32)
        low += jnp.dot(lower_part, onehot, preferred_element_type=F32)
    wanted = high.astype(jnp.int32) * 64 + low.astype(jnp.int32)
    words = pair_words(wanted)
    overflow = jnp.where(most > capacity, 1, 0)
    each = capacity // LANES
    for s in range(spaces):
        request_ref[s, 0:each, :] = words[s * each:(s + 1) * each]
        request_ref[s, each:, :] = jnp.broadcast_to(overflow, (ROWS - each, LANES))


def route(here, codes, spaces, per_space, capacity, interpret=False):
    return pl.pallas_call(
        functools.partial(route_kernel, capacity, per_space),
        out_shape=(
            jax.ShapeDtypeStruct((spaces, ROWS, LANES), jnp.int32),
            jax.ShapeDtypeStruct(codes.shape, jnp.int32),
        ),
        in_specs=[pl.BlockSpec(memory_space=pltpu.SMEM), pl.BlockSpec(memory_space=pltpu.VMEM)],
        out_specs=(pl.BlockSpec(memory_space=pltpu.VMEM), pl.BlockSpec(memory_space=pltpu.VMEM)),
        name="route",
        interpret=interpret,
    )(here, codes)


def pick_kernel(halves, row_tiles, words_ref, *refs):
    sources, outs = refs[:halves], refs[halves:]
    count = outs[0].shape[0]
    start = pl.program_id(0) * (count // row_tiles) * LANES
    lane = lax.broadcasted_iota(jnp.int32, (ROWS, LANES), 1)
    low = lane < TILE
    bit = jnp.where(low, 1 << 24, 1 << 25)

    for row in range(count // row_tiles):
        def tile(k, carry):
            word = words_ref[start + row * LANES + k * MAXB]
            swap = (jnp.broadcast_to(word, (ROWS, LANES)) & bit) != 0
            first = word & 0xFFF
            second = lax.shift_right_logical(word, 12) & 0xFFF
            for source_ref, out_ref in zip(sources, outs):
                a, b = source_ref[first], source_ref[second]
                crossed = jnp.where(low, b, a)
                crossed = jnp.concatenate([crossed[:, TILE:], crossed[:, :TILE]], axis=1)
                out_ref[row * row_tiles + k] = jnp.where(swap, crossed, jnp.where(low, a, b))
            return carry

        lax.fori_loop(0, row_tiles, tile, 0, unroll=16)


def pick(words, sources, row_tiles, interpret=False):
    count = words.shape[0] // LANES * row_tiles
    step = min(128, count)
    shape = jax.ShapeDtypeStruct((count, ROWS, LANES), BF16)
    return pl.pallas_call(
        functools.partial(pick_kernel, len(sources), row_tiles),
        out_shape=[shape] * len(sources),
        grid_spec=pltpu.PrefetchScalarGridSpec(
            num_scalar_prefetch=1,
            grid=(count // step,),
            in_specs=[
                pl.BlockSpec(source.shape, lambda i, words: (0, 0, 0), pipeline_mode=pl.Buffered(1))
                for source in sources
            ],
            out_specs=[pl.BlockSpec((step, ROWS, LANES), lambda i, words: (i, 0, 0))] * len(sources),
        ),
        compiler_params=pltpu.CompilerParams(vmem_limit_bytes=40 << 20),
        name="pick",
        interpret=interpret,
    )(words, *sources)


def project_kernel(group, counts_ref, first_ref, second_ref, weights_ref, basis_ref, remapped_ref, partial_ref):
    step = pl.program_id(0)

    @pl.when(step == 0)
    def _():
        partial_ref[...] = jnp.zeros_like(partial_ref)

    low = lax.broadcasted_iota(jnp.int32, (TILE, PAIR), 1) < TILE
    pieces = []
    for k in range(group):
        both = counts_ref[step * group + k] > 1
        weights = jnp.where(jnp.logical_or(low, both), weights_ref[k].astype(F32), 0.0).astype(BF16)
        picked = jnp.concatenate(
            [first_ref[:, k].reshape(-1, PAIR), second_ref[:, k].reshape(-1, PAIR)], axis=0
        )
        pieces.append(
            lax.dot_general(weights, picked, (((1,), (1,)), ((), ())), preferred_element_type=F32)
        )
    block = jnp.concatenate(pieces, axis=0).astype(BF16)
    remapped_ref[...] = block
    half = block.shape[1] // 2
    for c in range(2):
        add = jnp.dot(block[:, c * half:(c + 1) * half].T, basis_ref[...], preferred_element_type=F32)
        partial_ref[:, c] += add.reshape(half // ROWS, ROWS, -1)


def project(counts, arrived, weights, basis, interpret=False):
    owners = arrived[0].shape[0]
    snaps = owners * 2 * ROWS
    tiles = weights.shape[0]
    cells, rank = basis.shape
    group = 4
    chunk = pl.BlockSpec((owners, group, ROWS, PAIR), lambda i, counts: (0, i, 0, 0))
    return pl.pallas_call(
        functools.partial(project_kernel, group),
        out_shape=(
            jax.ShapeDtypeStruct((cells, snaps), BF16),
            jax.ShapeDtypeStruct((owners, 2, ROWS, rank), F32),
        ),
        grid_spec=pltpu.PrefetchScalarGridSpec(
            num_scalar_prefetch=1,
            grid=(tiles // group,),
            in_specs=[
                chunk,
                chunk,
                pl.BlockSpec((group, TILE, PAIR), lambda i, counts: (i, 0, 0)),
                pl.BlockSpec((group * TILE, rank), lambda i, counts: (i, 0)),
            ],
            out_specs=(
                pl.BlockSpec((group * TILE, snaps), lambda i, counts: (i, 0)),
                pl.BlockSpec((owners, 2, ROWS, rank), lambda i, counts: (0, 0, 0, 0)),
            ),
        ),
        compiler_params=pltpu.CompilerParams(vmem_limit_bytes=40 << 20),
        name="project",
        interpret=interpret,
    )(counts, *arrived, weights, basis)


def rotate_kernel(scale, remapped_ref, c0_ref, c1_ref, basis_ref, variances_ref, out_ref):
    half = c0_ref.shape[0]
    update = jnp.dot(remapped_ref[:, :half], c0_ref[...], preferred_element_type=F32)
    update += jnp.dot(remapped_ref[:, half:], c1_ref[...], preferred_element_type=F32)
    out_ref[...] = (basis_ref[...].astype(F32) * variances_ref[...] + update * scale).astype(BF16)


def rotate(remapped, halves, basis, variances, interpret=False):
    cells, rank = basis.shape
    snaps = remapped.shape[1]
    rows = min(256, cells)
    resident = lambda i: (0, 0)
    return pl.pallas_call(
        functools.partial(rotate_kernel, 1.0 / math.sqrt(snaps)),
        out_shape=jax.ShapeDtypeStruct((cells, rank), BF16),
        grid=(cells // rows,),
        in_specs=[
            pl.BlockSpec((rows, snaps), lambda i: (i, 0)),
            pl.BlockSpec((snaps // 2, rank), resident),
            pl.BlockSpec((snaps // 2, rank), resident),
            pl.BlockSpec((rows, rank), lambda i: (i, 0)),
            pl.BlockSpec((1, rank), resident),
        ],
        out_specs=pl.BlockSpec((rows, rank), lambda i: (i, 0)),
        compiler_params=pltpu.CompilerParams(vmem_limit_bytes=40 << 20),
        name="rotate",
        interpret=interpret,
    )(remapped, *halves, basis, variances[None, :])


def exchange(array, axis):
    return lax.all_to_all(array, axis, split_axis=0, concat_axis=0, tiled=True)


def spread(array, axis):
    return exchange(jnp.broadcast_to(array, (lax.axis_size(axis),) + array.shape), axis)


def per_device(interpret, capacity, snapshots, block_lists, tile_counts, remap_weights, basis, variances):
    tiles = block_lists.shape[0]
    owners, spaces = lax.axis_size("tm"), lax.axis_size("space")
    cells, rank = basis.shape
    total = cells * owners * spaces
    own_ranks = rank // spaces
    here = lax.axis_index("space")
    per_space = snapshots.shape[1] // TILE

    used = lax.broadcasted_iota(jnp.int32, block_lists.shape, 1) < tile_counts[:, None]
    codes = jnp.where(used, block_lists, -1).reshape(1, tiles * MAXB)
    codes = jnp.pad(codes, ((0, 0), (0, LANES - tiles * MAXB)), constant_values=-1)
    codes = spread(codes, "tm").reshape(owners, LANES)
    requests, local_words = route(here[None], codes, spaces, per_space, capacity, interpret)
    asked = exchange(requests, "space")
    each = capacity // LANES
    around = lax.dynamic_slice_in_dim(jnp.concatenate([asked, asked], axis=0), here, spaces, 0)
    asked_words = around[:, :each].reshape(-1)
    overflow = jnp.max(asked[:, each]) > 0
    halves_tiles = snapshots.reshape(2, ROWS, -1, LANES).transpose(0, 2, 1, 3)
    local = [halves_tiles[c] for c in range(2)]

    def finish(chosen):
        arrived = [exchange(c.reshape(owners, tiles, ROWS, PAIR), "tm") for c in chosen]
        remapped, partial = project(tile_counts, arrived, remap_weights, basis, interpret)
        parts = exchange(partial.reshape(owners, 2 * ROWS, rank), "tm")
        column = spread(jnp.sum(parts, axis=0), "space")
        coeffs = jnp.sum(column, axis=0) * (1.0 / math.sqrt(total))
        half = coeffs.astype(BF16)
        rest = lax.dynamic_slice_in_dim(coeffs - half.astype(F32), here * own_ranks, own_ranks, 1)
        everyone = spread(jnp.concatenate([half, rest.astype(BF16)], axis=1), "tm")
        halves = [
            everyone[:, c * ROWS:(c + 1) * ROWS, :rank].reshape(owners * ROWS, rank) for c in range(2)
        ]
        high = lax.dynamic_slice_in_dim(everyone, here * own_ranks, own_ranks, 2)
        own = high.astype(F32) + everyone[:, :, rank:].astype(F32)
        own_coeffs = own.reshape(owners * 2 * ROWS, own_ranks).T
        return own_coeffs, rotate(remapped, halves, basis, variances, interpret)

    def dense():
        blocks = jnp.maximum(codes, 0)
        words = pair_words_plain(blocks).reshape(-1)
        sources = [spread(c, "space").reshape(-1, ROWS, LANES) for c in local]
        return finish([pick(words, [source], tiles, interpret)[0] for source in sources])

    def sparse():
        sent = pick(asked_words, local, LANES // MAXB, interpret)
        came = []
        for c in sent:
            c = c.reshape(spaces, -1, ROWS, LANES)
            parts = [c[0]] + [
                lax.ppermute(c[d], "space", [(i, (i + d) % spaces) for i in range(spaces)])
                for d in range(1, spaces)
            ]
            came.append(jnp.concatenate(parts, axis=0))
        words = local_words.reshape(-1)
        chosen = []
        for c in came:
            chosen += pick(words, [c.reshape(-1, ROWS, LANES)], tiles, interpret)
        return finish(chosen)

    return lax.cond(overflow, dense, sparse)


def pair_words_plain(index):
    after = jnp.roll(index, -1, axis=1)
    return (index >> 1) | ((after >> 1) << 12) | ((index & 1) << 24) | ((1 - (after & 1)) << 25)


def solution(mesh, interpret=False, capacity=CAPACITY):
    return jax.shard_map(
        functools.partial(per_device, interpret, capacity),
        mesh=mesh,
        in_specs=(
            P("tm", "space"),
            P(("tm", "space"), None),
            P(("tm", "space")),
            P(("tm", "space"), None, None),
            P(("tm", "space"), None),
            P(),
        ),
        out_specs=(P("space", None), P(("tm", "space"), None)),
        check_vma=False,
    )
```

```python
import functools
import math

import jax
import jax.numpy as jnp
from jax import lax
from jax.experimental import pallas as pl
from jax.experimental.pallas import tpu as pltpu
from jax.sharding import PartitionSpec as P


TILE = 64
MAXB = 2
PAIR = MAXB * TILE
ROWS = 8
LANES = 128
CAPACITY = 256
BF16 = jnp.bfloat16
F32 = jnp.float32


def pair_words(index):
    after = pltpu.roll(index, LANES - 1, 1)
    return (
        lax.shift_right_logical(index, 1)
        | (lax.shift_right_logical(after, 1) << 12)
        | ((index & 1) << 24)
        | ((1 - (after & 1)) << 25)
    )


def route_kernel(capacity, per_space, here_ref, codes_ref, request_ref, local_ref):
    owners = codes_ref.shape[0]
    spaces = request_ref.shape[0]
    here = here_ref[0]
    codes = codes_ref[...]
    owner_of = jnp.where(codes < 0, -1, lax.div(jnp.maximum(codes, 0), per_space))
    within = jnp.where(codes < 0, 0, lax.rem(jnp.maximum(codes, 0), per_space))
    upper = lax.broadcasted_iota(jnp.int32, (LANES, LANES), 0) <= lax.broadcasted_iota(jnp.int32, (LANES, LANES), 1)
    upper = jnp.where(upper, 1.0, 0.0).astype(BF16)
    lower = lax.broadcasted_iota(jnp.int32, (owners, owners), 0) > lax.broadcasted_iota(jnp.int32, (owners, owners), 1)
    lower = jnp.where(lower, 1.0, 0.0).astype(BF16)
    location = jnp.zeros_like(codes)
    target = jnp.full_like(codes, -1)
    most = jnp.zeros((1, LANES), F32)
    for s in range(spaces):
        match = owner_of == s
        ones = jnp.where(match, 1.0, 0.0).astype(BF16)
        prefix = jnp.dot(ones, upper, preferred_element_type=F32)
        sums = jnp.broadcast_to(prefix[:, LANES - 1:], (owners, LANES))
        ahead = jnp.dot(lower, sums.astype(BF16), preferred_element_type=F32)
        rank = (prefix + ahead).astype(jnp.int32) - 1
        most = jnp.maximum(most, ahead[owners - 1:] + sums[owners - 1:])
        location = jnp.where(match, rank + lax.rem(here - s + spaces, spaces) * capacity, location)
        target = jnp.where(match, rank + s * capacity, target)
    local_ref[...] = pair_words(location)

    rows = spaces * capacity // LANES
    row_id = lax.broadcasted_iota(jnp.int32, (rows, LANES), 0)
    lane_id = lax.broadcasted_iota(jnp.int32, (LANES, LANES), 1)
    lane_of = (target & (LANES - 1)).astype(F32)
    lane_of = jnp.concatenate([lane_of, jnp.zeros((LANES - owners, LANES), F32)], axis=0).T
    high = jnp.zeros((rows, LANES), F32)
    low = jnp.zeros((rows, LANES), F32)
    for r in range(owners):
        hit = jnp.broadcast_to(target[r:r + 1] >> 7, (rows, LANES)) == row_id
        value = jnp.broadcast_to(within[r:r + 1], (rows, LANES))
        upper_part = jnp.where(hit, lax.shift_right_logical(value, 6), 0).astype(F32).astype(BF16)
        lower_part = jnp.where(hit, value & 63, 0).astype(F32).astype(BF16)
        column = jnp.broadcast_to(lane_of[:, r:r + 1], (LANES, LANES)).astype(jnp.int32)
        onehot = jnp.where(column == lane_id, 1.0, 0.0).astype(BF16)
        high += jnp.dot(upper_part, onehot, preferred_element_type=F32)
        low += jnp.dot(lower_part, onehot, preferred_element_type=F32)
    wanted = high.astype(jnp.int32) * 64 + low.astype(jnp.int32)
    words = pair_words(wanted)
    overflow = jnp.where(most > capacity, 1, 0)
    each = capacity // LANES
    for s in range(spaces):
        request_ref[s, 0:each, :] = words[s * each:(s + 1) * each]
        request_ref[s, each:, :] = jnp.broadcast_to(overflow, (ROWS - each, LANES))


def route(here, codes, spaces, per_space, capacity, interpret=False):
    return pl.pallas_call(
        functools.partial(route_kernel, capacity, per_space),
        out_shape=(
            jax.ShapeDtypeStruct((spaces, ROWS, LANES), jnp.int32),
            jax.ShapeDtypeStruct(codes.shape, jnp.int32),
        ),
        in_specs=[pl.BlockSpec(memory_space=pltpu.SMEM), pl.BlockSpec(memory_space=pltpu.VMEM)],
        out_specs=(pl.BlockSpec(memory_space=pltpu.VMEM), pl.BlockSpec(memory_space=pltpu.VMEM)),
        name="route",
        interpret=interpret,
    )(here, codes)


def pick_kernel(halves, parts, row_tiles, words_ref, *refs):
    inputs, rest = refs[:halves * parts], refs[halves * parts:]
    outs, sources, sems = rest[:halves], rest[halves:2 * halves], rest[2 * halves]
    count = outs[0].shape[0]
    start = pl.program_id(0) * (count // row_tiles) * LANES
    lane = lax.broadcasted_iota(jnp.int32, (ROWS, LANES), 1)
    low = lane < TILE
    bit = jnp.where(low, 1 << 24, 1 << 25)

    @pl.when(pl.program_id(0) == 0)
    def _():
        size = sources[0].shape[0] // parts
        copies = [
            pltpu.make_async_copy(
                inputs[h * parts + p], sources[h].at[pl.ds(p * size, size)], sems.at[h * parts + p]
            )
            for h in range(halves)
            for p in range(parts)
        ]
        for copy in copies:
            copy.start()
        for copy in copies:
            copy.wait()

    for row in range(count // row_tiles):
        def tile(k, carry):
            word = words_ref[start + row * LANES + k * MAXB]
            swap = (jnp.broadcast_to(word, (ROWS, LANES)) & bit) != 0
            first = word & 0xFFF
            second = lax.shift_right_logical(word, 12) & 0xFFF
            for source_ref, out_ref in zip(sources, outs):
                a, b = source_ref[first], source_ref[second]
                crossed = jnp.where(low, b, a)
                crossed = jnp.concatenate([crossed[:, TILE:], crossed[:, :TILE]], axis=1)
                out_ref[row * row_tiles + k] = jnp.where(swap, crossed, jnp.where(low, a, b))
            return carry

        lax.fori_loop(0, row_tiles, tile, 0, unroll=16)


def in_hbm(shape, dtype, interpret):
    return jax.ShapeDtypeStruct(shape, dtype) if interpret else pltpu.HBM(shape, dtype)


def pick(words, sources, row_tiles, interpret=False):
    count = words.shape[0] // LANES * row_tiles
    step = min(128, count)
    halves, parts = len(sources), len(sources[0])
    size = parts * sources[0][0].shape[0]
    return pl.pallas_call(
        functools.partial(pick_kernel, halves, parts, row_tiles),
        out_shape=[in_hbm((count, ROWS, LANES), BF16, interpret)] * halves,
        grid_spec=pltpu.PrefetchScalarGridSpec(
            num_scalar_prefetch=1,
            grid=(count // step,),
            in_specs=[pl.BlockSpec(memory_space=pl.ANY)] * (halves * parts),
            out_specs=[pl.BlockSpec((step, ROWS, LANES), lambda i, words: (i, 0, 0))] * halves,
            scratch_shapes=[pltpu.VMEM((size, ROWS, LANES), BF16)] * halves
            + [pltpu.SemaphoreType.DMA((halves * parts,))],
        ),
        compiler_params=pltpu.CompilerParams(vmem_limit_bytes=40 << 20),
        name="pick",
        interpret=interpret,
    )(words, *[part for source in sources for part in source])


def project_kernel(group, counts_ref, first_ref, second_ref, weights_ref, basis_ref, remapped_ref, partial_ref):
    step = pl.program_id(0)

    @pl.when(step == 0)
    def _():
        partial_ref[...] = jnp.zeros_like(partial_ref)

    low = lax.broadcasted_iota(jnp.int32, (TILE, PAIR), 1) < TILE
    pieces = []
    for k in range(group):
        both = counts_ref[step * group + k] > 1
        weights = jnp.where(jnp.logical_or(low, both), weights_ref[k].astype(F32), 0.0).astype(BF16)
        picked = jnp.concatenate(
            [first_ref[:, k].reshape(-1, PAIR), second_ref[:, k].reshape(-1, PAIR)], axis=0
        )
        pieces.append(
            lax.dot_general(weights, picked, (((1,), (1,)), ((), ())), preferred_element_type=F32)
        )
    block = jnp.concatenate(pieces, axis=0).astype(BF16)
    remapped_ref[...] = block
    half = block.shape[1] // 2
    for c in range(2):
        add = jnp.dot(block[:, c * half:(c + 1) * half].T, basis_ref[...], preferred_element_type=F32)
        partial_ref[:, c] += add.reshape(half // ROWS, ROWS, -1)


def project(counts, arrived, weights, basis, interpret=False):
    owners = arrived[0].shape[0]
    snaps = owners * 2 * ROWS
    tiles = weights.shape[0]
    cells, rank = basis.shape
    group = 4
    chunk = pl.BlockSpec((owners, group, ROWS, PAIR), lambda i, counts: (0, i, 0, 0))
    return pl.pallas_call(
        functools.partial(project_kernel, group),
        out_shape=(
            in_hbm((cells, snaps), BF16, interpret),
            in_hbm((owners, 2, ROWS, rank), F32, interpret),
        ),
        grid_spec=pltpu.PrefetchScalarGridSpec(
            num_scalar_prefetch=1,
            grid=(tiles // group,),
            in_specs=[
                chunk,
                chunk,
                pl.BlockSpec((group, TILE, PAIR), lambda i, counts: (i, 0, 0)),
                pl.BlockSpec((group * TILE, rank), lambda i, counts: (i, 0)),
            ],
            out_specs=(
                pl.BlockSpec((group * TILE, snaps), lambda i, counts: (i, 0)),
                pl.BlockSpec((owners, 2, ROWS, rank), lambda i, counts: (0, 0, 0, 0)),
            ),
        ),
        compiler_params=pltpu.CompilerParams(vmem_limit_bytes=40 << 20),
        name="project",
        interpret=interpret,
    )(counts, *arrived, weights, basis)


def rotate_kernel(scale, remapped_ref, c0_ref, c1_ref, basis_ref, variances_ref, out_ref):
    half = c0_ref.shape[0]
    update = jnp.dot(remapped_ref[:, :half], c0_ref[...], preferred_element_type=F32)
    update += jnp.dot(remapped_ref[:, half:], c1_ref[...], preferred_element_type=F32)
    out_ref[...] = (basis_ref[...].astype(F32) * variances_ref[...] + update * scale).astype(BF16)


def rotate(remapped, halves, basis, variances, interpret=False):
    cells, rank = basis.shape
    snaps = remapped.shape[1]
    rows = min(256, cells)
    resident = lambda i: (0, 0)
    return pl.pallas_call(
        functools.partial(rotate_kernel, 1.0 / math.sqrt(snaps)),
        out_shape=in_hbm((cells, rank), BF16, interpret),
        grid=(cells // rows,),
        in_specs=[
            pl.BlockSpec((rows, snaps), lambda i: (i, 0)),
            pl.BlockSpec((snaps // 2, rank), resident),
            pl.BlockSpec((snaps // 2, rank), resident),
            pl.BlockSpec((rows, rank), lambda i: (i, 0)),
            pl.BlockSpec((1, rank), resident),
        ],
        out_specs=pl.BlockSpec((rows, rank), lambda i: (i, 0)),
        compiler_params=pltpu.CompilerParams(vmem_limit_bytes=40 << 20),
        name="rotate",
        interpret=interpret,
    )(remapped, *halves, basis, variances[None, :])


def exchange(array, axis):
    return lax.all_to_all(array, axis, split_axis=0, concat_axis=0, tiled=True)


def spread(array, axis):
    return exchange(jnp.broadcast_to(array, (lax.axis_size(axis),) + array.shape), axis)


def per_device(interpret, capacity, snapshots, block_lists, tile_counts, remap_weights, basis, variances):
    tiles = block_lists.shape[0]
    owners, spaces = lax.axis_size("tm"), lax.axis_size("space")
    cells, rank = basis.shape
    total = cells * owners * spaces
    own_ranks = rank // spaces
    here = lax.axis_index("space")
    per_space = snapshots.shape[1] // TILE

    used = lax.broadcasted_iota(jnp.int32, block_lists.shape, 1) < tile_counts[:, None]
    codes = jnp.where(used, block_lists, -1).reshape(1, tiles * MAXB)
    codes = jnp.pad(codes, ((0, 0), (0, LANES - tiles * MAXB)), constant_values=-1)
    codes = spread(codes, "tm").reshape(owners, LANES)
    requests, local_words = route(here[None], codes, spaces, per_space, capacity, interpret)
    asked = exchange(requests, "space")
    each = capacity // LANES
    around = lax.dynamic_slice_in_dim(jnp.concatenate([asked, asked], axis=0), here, spaces, 0)
    asked_words = around[:, :each].reshape(-1)
    overflow = jnp.max(asked[:, each]) > 0
    halves_tiles = snapshots.reshape(2, ROWS, -1, LANES).transpose(0, 2, 1, 3)
    local = [halves_tiles[c] for c in range(2)]

    def finish(chosen):
        arrived = [exchange(c.reshape(owners, tiles, ROWS, PAIR), "tm") for c in chosen]
        remapped, partial = project(tile_counts, arrived, remap_weights, basis, interpret)
        parts = exchange(partial.reshape(owners, 2 * ROWS, rank), "tm")
        column = spread(jnp.sum(parts, axis=0), "space")
        coeffs = jnp.sum(column, axis=0) * (1.0 / math.sqrt(total))
        half = coeffs.astype(BF16)
        rest = lax.dynamic_slice_in_dim(coeffs - half.astype(F32), here * own_ranks, own_ranks, 1)
        everyone = spread(jnp.concatenate([half, rest.astype(BF16)], axis=1), "tm")
        halves = [
            everyone[:, c * ROWS:(c + 1) * ROWS, :rank].reshape(owners * ROWS, rank) for c in range(2)
        ]
        high = lax.dynamic_slice_in_dim(everyone, here * own_ranks, own_ranks, 2)
        own = high.astype(F32) + everyone[:, :, rank:].astype(F32)
        own_coeffs = own.reshape(owners * 2 * ROWS, own_ranks).T
        return own_coeffs, rotate(remapped, halves, basis, variances, interpret)

    def dense():
        blocks = jnp.maximum(codes, 0)
        words = pair_words_plain(blocks).reshape(-1)
        sources = [spread(c, "space").reshape(-1, ROWS, LANES) for c in local]
        return finish([pick(words, [[source]], tiles, interpret)[0] for source in sources])

    def sparse():
        sent = pick(asked_words, [[c] for c in local], LANES // MAXB, interpret)
        came = []
        for c in sent:
            c = c.reshape(spaces, -1, ROWS, LANES)
            parts = [c[0]] + [
                lax.ppermute(c[d], "space", [(i, (i + d) % spaces) for i in range(spaces)])
                for d in range(1, spaces)
            ]
            came.append(parts)
        words = local_words.reshape(-1)
        chosen = []
        for c in came:
            chosen += pick(words, [c], tiles, interpret)
        return finish(chosen)

    return lax.cond(overflow, dense, sparse)


def pair_words_plain(index):
    after = jnp.roll(index, -1, axis=1)
    return (index >> 1) | ((after >> 1) << 12) | ((index & 1) << 24) | ((1 - (after & 1)) << 25)


def solution(mesh, interpret=False, capacity=CAPACITY):
    return jax.shard_map(
        functools.partial(per_device, interpret, capacity),
        mesh=mesh,
        in_specs=(
            P("tm", "space"),
            P(("tm", "space"), None),
            P(("tm", "space")),
            P(("tm", "space"), None, None),
            P(("tm", "space"), None),
            P(),
        ),
        out_specs=(P("space", None), P(("tm", "space"), None)),
        check_vma=False,
    )
```

```python
import functools
import math

import jax
import jax.numpy as jnp
from jax import lax
from jax.experimental import pallas as pl
from jax.experimental.pallas import tpu as pltpu
from jax.sharding import PartitionSpec as P


TILE = 64
MAXB = 2
PAIR = MAXB * TILE
ROWS = 8
LANES = 128
CAPACITY = 256
UNROLL = 16
BF16 = jnp.bfloat16
F32 = jnp.float32


def pair_words(index):
    after = pltpu.roll(index, LANES - 1, 1)
    return (
        lax.shift_right_logical(index, 1)
        | (lax.shift_right_logical(after, 1) << 12)
        | ((index & 1) << 24)
        | ((1 - (after & 1)) << 25)
    )


def route_kernel(capacity, per_space, here_ref, codes_ref, request_ref, local_ref):
    owners = codes_ref.shape[0]
    spaces = request_ref.shape[0]
    here = here_ref[0]
    codes = codes_ref[...]
    owner_of = jnp.where(codes < 0, -1, lax.div(jnp.maximum(codes, 0), per_space))
    within = jnp.where(codes < 0, 0, lax.rem(jnp.maximum(codes, 0), per_space))
    upper = lax.broadcasted_iota(jnp.int32, (LANES, LANES), 0) <= lax.broadcasted_iota(jnp.int32, (LANES, LANES), 1)
    upper = jnp.where(upper, 1.0, 0.0).astype(BF16)
    lower = lax.broadcasted_iota(jnp.int32, (owners, owners), 0) > lax.broadcasted_iota(jnp.int32, (owners, owners), 1)
    lower = jnp.where(lower, 1.0, 0.0).astype(BF16)
    location = jnp.zeros_like(codes)
    target = jnp.full_like(codes, -1)
    most = jnp.zeros((1, LANES), F32)
    for s in range(spaces):
        match = owner_of == s
        ones = jnp.where(match, 1.0, 0.0).astype(BF16)
        prefix = jnp.dot(ones, upper, preferred_element_type=F32)
        sums = jnp.broadcast_to(prefix[:, LANES - 1:], (owners, LANES))
        ahead = jnp.dot(lower, sums.astype(BF16), preferred_element_type=F32)
        rank = (prefix + ahead).astype(jnp.int32) - 1
        most = jnp.maximum(most, ahead[owners - 1:] + sums[owners - 1:])
        location = jnp.where(match, rank + lax.rem(here - s + spaces, spaces) * capacity, location)
        target = jnp.where(match, rank + s * capacity, target)
    local_ref[...] = pair_words(location)

    rows = spaces * capacity // LANES
    row_id = lax.broadcasted_iota(jnp.int32, (rows, LANES), 0)
    lane_id = lax.broadcasted_iota(jnp.int32, (LANES, LANES), 1)
    lane_of = (target & (LANES - 1)).astype(F32)
    lane_of = jnp.concatenate([lane_of, jnp.zeros((LANES - owners, LANES), F32)], axis=0).T
    high = jnp.zeros((rows, LANES), F32)
    low = jnp.zeros((rows, LANES), F32)
    for r in range(owners):
        hit = jnp.broadcast_to(target[r:r + 1] >> 7, (rows, LANES)) == row_id
        value = jnp.broadcast_to(within[r:r + 1], (rows, LANES))
        upper_part = jnp.where(hit, lax.shift_right_logical(value, 6), 0).astype(F32).astype(BF16)
        lower_part = jnp.where(hit, value & 63, 0).astype(F32).astype(BF16)
        column = jnp.broadcast_to(lane_of[:, r:r + 1], (LANES, LANES)).astype(jnp.int32)
        onehot = jnp.where(column == lane_id, 1.0, 0.0).astype(BF16)
        high += jnp.dot(upper_part, onehot, preferred_element_type=F32)
        low += jnp.dot(lower_part, onehot, preferred_element_type=F32)
    wanted = high.astype(jnp.int32) * 64 + low.astype(jnp.int32)
    words = pair_words(wanted)
    overflow = jnp.where(most > capacity, 1, 0)
    each = capacity // LANES
    for s in range(spaces):
        request_ref[s, 0:each, :] = words[s * each:(s + 1) * each]
        request_ref[s, each:, :] = jnp.broadcast_to(overflow, (ROWS - each, LANES))


def route(here, codes, spaces, per_space, capacity, interpret=False):
    return pl.pallas_call(
        functools.partial(route_kernel, capacity, per_space),
        out_shape=(
            jax.ShapeDtypeStruct((spaces, ROWS, LANES), jnp.int32),
            jax.ShapeDtypeStruct(codes.shape, jnp.int32),
        ),
        in_specs=[pl.BlockSpec(memory_space=pltpu.SMEM), pl.BlockSpec(memory_space=pltpu.VMEM)],
        out_specs=(pl.BlockSpec(memory_space=pltpu.VMEM), pl.BlockSpec(memory_space=pltpu.VMEM)),
        name="route",
        interpret=interpret,
    )(here, codes)


def lane_masks():
    low = lax.broadcasted_iota(jnp.int32, (ROWS, LANES), 1) < TILE
    return low, jnp.where(low, 1 << 24, 1 << 25)


def joined(word, source_ref, low, bit):
    a = source_ref[word & 0xFFF]
    b = source_ref[lax.shift_right_logical(word, 12) & 0xFFF]
    swap = (jnp.broadcast_to(word, (ROWS, LANES)) & bit) != 0
    crossed = jnp.where(low, b, a)
    crossed = jnp.concatenate([crossed[:, TILE:], crossed[:, :TILE]], axis=1)
    return jnp.where(swap, crossed, jnp.where(low, a, b))


def pick_kernel(row_tiles, words_ref, *refs):
    out_ref, source_ref, sems = refs[-3:]
    inputs = refs[:-3]
    start = pl.program_id(0) * (out_ref.shape[0] // row_tiles) * LANES
    low, bit = lane_masks()

    @pl.when(pl.program_id(0) == 0)
    def _():
        size = source_ref.shape[0] // len(inputs)
        copies = [
            pltpu.make_async_copy(part, source_ref.at[pl.ds(p * size, size)], sems.at[p])
            for p, part in enumerate(inputs)
        ]
        for copy in copies:
            copy.start()
        for copy in copies:
            copy.wait()

    for row in range(out_ref.shape[0] // row_tiles):
        def tile(k, carry):
            word = words_ref[start + row * LANES + k * MAXB]
            out_ref[row * row_tiles + k] = joined(word, source_ref, low, bit)
            return carry

        lax.fori_loop(0, row_tiles, tile, 0, unroll=min(UNROLL, row_tiles))


def gather_kernel(pitch, words_ref, input_ref, *refs):
    outs, (source_ref, sem) = refs[:-2], refs[-2:]
    low, bit = lane_masks()
    copy = pltpu.make_async_copy(input_ref, source_ref, sem)
    copy.start()
    copy.wait()
    for d, out_ref in enumerate(outs):
        def tile(k, carry):
            out_ref[k] = joined(words_ref[d * pitch + k * MAXB], source_ref, low, bit)
            return carry

        lax.fori_loop(0, out_ref.shape[0], tile, 0, unroll=UNROLL)


def gather(words, source, spaces, capacity, interpret=False):
    shape = (capacity // MAXB, ROWS, LANES)
    return pl.pallas_call(
        functools.partial(gather_kernel, words.shape[0] // spaces),
        out_shape=[jax.ShapeDtypeStruct(shape, BF16)] * spaces,
        grid_spec=pltpu.PrefetchScalarGridSpec(
            num_scalar_prefetch=1,
            grid=(1,),
            in_specs=[pl.BlockSpec(memory_space=pl.ANY)],
            out_specs=[pl.BlockSpec(shape, lambda i, words: (0, 0, 0))] * spaces,
            scratch_shapes=[pltpu.VMEM(source.shape, BF16), pltpu.SemaphoreType.DMA],
        ),
        compiler_params=pltpu.CompilerParams(vmem_limit_bytes=40 << 20),
        name="gather",
        interpret=interpret,
    )(words, source)


def in_hbm(shape, dtype, interpret):
    return jax.ShapeDtypeStruct(shape, dtype) if interpret else pltpu.HBM(shape, dtype)


def pick(words, parts, row_tiles, interpret=False):
    count = words.shape[0] // LANES * row_tiles
    step = min(128, count)
    size = len(parts) * parts[0].shape[0]
    return pl.pallas_call(
        functools.partial(pick_kernel, row_tiles),
        out_shape=in_hbm((count, ROWS, LANES), BF16, interpret),
        grid_spec=pltpu.PrefetchScalarGridSpec(
            num_scalar_prefetch=1,
            grid=(count // step,),
            in_specs=[pl.BlockSpec(memory_space=pl.ANY)] * len(parts),
            out_specs=pl.BlockSpec((step, ROWS, LANES), lambda i, words: (i, 0, 0)),
            scratch_shapes=[
                pltpu.VMEM((size, ROWS, LANES), BF16),
                pltpu.SemaphoreType.DMA((len(parts),)),
            ],
        ),
        compiler_params=pltpu.CompilerParams(vmem_limit_bytes=40 << 20),
        name="pick",
        interpret=interpret,
    )(words, *parts)


def project_kernel(group, counts_ref, first_ref, second_ref, weights_ref, basis_ref, remapped_ref, rounded_ref, partial_ref):
    step = pl.program_id(0)

    @pl.when(step == 0)
    def _():
        partial_ref[...] = jnp.zeros_like(partial_ref)

    low = lax.broadcasted_iota(jnp.int32, (TILE, PAIR), 1) < TILE
    pieces = []
    for k in range(group):
        both = counts_ref[step * group + k] > 1
        weights = jnp.where(jnp.logical_or(low, both), weights_ref[k].astype(F32), 0.0).astype(BF16)
        picked = jnp.concatenate(
            [first_ref[:, k].reshape(-1, PAIR), second_ref[:, k].reshape(-1, PAIR)], axis=0
        )
        pieces.append(
            lax.dot_general(weights, picked, (((1,), (1,)), ((), ())), preferred_element_type=F32)
        )
    block = jnp.concatenate(pieces, axis=0).astype(BF16)
    remapped_ref[...] = block
    half = block.shape[1] // 2
    for c in range(2):
        add = jnp.dot(block[:, c * half:(c + 1) * half].T, basis_ref[...], preferred_element_type=F32)
        partial_ref[:, c] += add.reshape(half // ROWS, ROWS, -1)

    @pl.when(step == pl.num_programs(0) - 1)
    def _():
        rounded_ref[...] = partial_ref[...].astype(BF16)


def project(counts, arrived, weights, basis, interpret=False):
    owners = arrived[0].shape[0]
    snaps = owners * 2 * ROWS
    tiles = weights.shape[0]
    cells, rank = basis.shape
    group = 4
    chunk = pl.BlockSpec((owners, group, ROWS, PAIR), lambda i, counts: (0, i, 0, 0))
    return pl.pallas_call(
        functools.partial(project_kernel, group),
        out_shape=(
            in_hbm((cells, snaps), BF16, interpret),
            jax.ShapeDtypeStruct((owners, 2, ROWS, rank), BF16),
        ),
        grid_spec=pltpu.PrefetchScalarGridSpec(
            num_scalar_prefetch=1,
            grid=(tiles // group,),
            in_specs=[
                chunk,
                chunk,
                pl.BlockSpec((group, TILE, PAIR), lambda i, counts: (i, 0, 0)),
                pl.BlockSpec((group * TILE, rank), lambda i, counts: (i, 0)),
            ],
            out_specs=(
                pl.BlockSpec((group * TILE, snaps), lambda i, counts: (i, 0)),
                pl.BlockSpec((owners, 2, ROWS, rank), lambda i, counts: (0, 0, 0, 0)),
            ),
            scratch_shapes=[pltpu.VMEM((owners, 2, ROWS, rank), F32)],
        ),
        compiler_params=pltpu.CompilerParams(vmem_limit_bytes=40 << 20),
        name="project",
        interpret=interpret,
    )(counts, *arrived, weights, basis)


def rotate_kernel(scale, remapped_ref, c0_ref, c1_ref, basis_ref, variances_ref, out_ref):
    half = c0_ref.shape[0]
    update = jnp.dot(remapped_ref[:, :half], c0_ref[...], preferred_element_type=F32)
    update += jnp.dot(remapped_ref[:, half:], c1_ref[...], preferred_element_type=F32)
    out_ref[...] = (basis_ref[...].astype(F32) * variances_ref[...] + update * scale).astype(BF16)


def rotate(remapped, halves, basis, variances, interpret=False):
    cells, rank = basis.shape
    snaps = remapped.shape[1]
    rows = min(256, cells)
    resident = lambda i: (0, 0)
    return pl.pallas_call(
        functools.partial(rotate_kernel, 1.0 / math.sqrt(snaps)),
        out_shape=in_hbm((cells, rank), BF16, interpret),
        grid=(cells // rows,),
        in_specs=[
            pl.BlockSpec((rows, snaps), lambda i: (i, 0)),
            pl.BlockSpec((snaps // 2, rank), resident),
            pl.BlockSpec((snaps // 2, rank), resident),
            pl.BlockSpec((rows, rank), lambda i: (i, 0)),
            pl.BlockSpec((1, rank), resident),
        ],
        out_specs=pl.BlockSpec((rows, rank), lambda i: (i, 0)),
        compiler_params=pltpu.CompilerParams(vmem_limit_bytes=40 << 20),
        name="rotate",
        interpret=interpret,
    )(remapped, *halves, basis, variances[None, :])


def exchange(array, axis):
    return lax.all_to_all(array, axis, split_axis=0, concat_axis=0, tiled=True)


def spread(array, axis):
    return exchange(jnp.broadcast_to(array, (lax.axis_size(axis),) + array.shape), axis)


def per_device(interpret, capacity, snapshots, block_lists, tile_counts, remap_weights, basis, variances):
    tiles = block_lists.shape[0]
    owners, spaces = lax.axis_size("tm"), lax.axis_size("space")
    cells, rank = basis.shape
    total = cells * owners * spaces
    own_ranks = rank // spaces
    here = lax.axis_index("space")
    per_space = snapshots.shape[1] // TILE

    used = lax.broadcasted_iota(jnp.int32, block_lists.shape, 1) < tile_counts[:, None]
    codes = jnp.where(used, block_lists, -1).reshape(1, tiles * MAXB)
    codes = jnp.pad(codes, ((0, 0), (0, LANES - tiles * MAXB)), constant_values=-1)
    codes = spread(codes, "tm").reshape(owners, LANES)
    requests, local_words = route(here[None], codes, spaces, per_space, capacity, interpret)
    asked = exchange(requests, "space")
    each = capacity // LANES
    around = lax.dynamic_slice_in_dim(jnp.concatenate([asked, asked], axis=0), here, spaces, 0)
    asked_words = around[:, :each].reshape(-1)
    overflow = jnp.max(asked[:, each]) > 0
    halves_tiles = snapshots.reshape(2, ROWS, -1, LANES).transpose(0, 2, 1, 3)
    local = [halves_tiles[c] for c in range(2)]

    def finish(chosen):
        arrived = [exchange(c.reshape(owners, tiles, ROWS, PAIR), "tm") for c in chosen]
        remapped, partial = project(tile_counts, arrived, remap_weights, basis, interpret)
        parts = exchange(partial.reshape(owners, 2 * ROWS, rank), "tm")
        column = spread(jnp.sum(parts.astype(F32), axis=0), "space")
        coeffs = jnp.sum(column, axis=0) * (1.0 / math.sqrt(total))
        half = coeffs.astype(BF16)
        rest = lax.dynamic_slice_in_dim(coeffs - half.astype(F32), here * own_ranks, own_ranks, 1)
        everyone = spread(jnp.concatenate([half, rest.astype(BF16)], axis=1), "tm")
        halves = [
            everyone[:, c * ROWS:(c + 1) * ROWS, :rank].reshape(owners * ROWS, rank) for c in range(2)
        ]
        high = lax.dynamic_slice_in_dim(everyone, here * own_ranks, own_ranks, 2)
        own = high.astype(F32) + everyone[:, :, rank:].astype(F32)
        own_coeffs = own.reshape(owners * 2 * ROWS, own_ranks).T
        return own_coeffs, rotate(remapped, halves, basis, variances, interpret)

    def dense():
        blocks = jnp.maximum(codes, 0)
        words = pair_words_plain(blocks).reshape(-1)
        sources = [spread(c, "space").reshape(-1, ROWS, LANES) for c in local]
        return finish([pick(words, [source], tiles, interpret) for source in sources])

    def sparse():
        came = []
        for source in local:
            sent = gather(asked_words, source, spaces, capacity, interpret)
            came.append([sent[0]] + [
                lax.ppermute(sent[d], "space", [(j, (j + d) % spaces) for j in range(spaces)])
                for d in range(1, spaces)
            ])
        words = local_words.reshape(-1)
        chosen = []
        for c in came:
            chosen.append(pick(words, c, tiles, interpret))
        return finish(chosen)

    return lax.cond(overflow, dense, sparse)


def pair_words_plain(index):
    after = jnp.roll(index, -1, axis=1)
    return (index >> 1) | ((after >> 1) << 12) | ((index & 1) << 24) | ((1 - (after & 1)) << 25)


def solution(mesh, interpret=False, capacity=CAPACITY):
    return jax.shard_map(
        functools.partial(per_device, interpret, capacity),
        mesh=mesh,
        in_specs=(
            P("tm", "space"),
            P(("tm", "space"), None),
            P(("tm", "space")),
            P(("tm", "space"), None, None),
            P(("tm", "space"), None),
            P(),
        ),
        out_specs=(P("space", None), P(("tm", "space"), None)),
        check_vma=False,
    )
```

```python
import functools
import math

import jax
import jax.numpy as jnp
from jax import lax
from jax.experimental import pallas as pl
from jax.experimental.pallas import tpu as pltpu
from jax.sharding import PartitionSpec as P


TILE = 64
MAXB = 2
PAIR = MAXB * TILE
ROWS = 8
LANES = 128
LIMITS = (112, 200, 256)
SHARES = (12, 24, 32)
BF16 = jnp.bfloat16
F32 = jnp.float32


def pair_words(index):
    after = pltpu.roll(index, LANES - 1, 1)
    return (
        lax.shift_right_logical(index, 1)
        | (lax.shift_right_logical(after, 1) << 12)
        | ((index & 1) << 24)
        | ((1 - (after & 1)) << 25)
    )


def staged(values, edges, at):
    result = values[-1]
    for value, edge in reversed(list(zip(values[:-1], edges[:-1]))):
        result = jnp.where(at < edge, value, result)
    return result


def route_kernel(limits, edges, per_space, here_ref, codes_ref, request_ref, local_ref):
    owners = codes_ref.shape[0]
    spaces = request_ref.shape[0]
    pitch = -(-limits[-1] // LANES) * LANES
    here = here_ref[0]
    codes = codes_ref[...]
    owner_of = jnp.where(codes < 0, -1, lax.div(jnp.maximum(codes, 0), per_space))
    within = jnp.where(codes < 0, 0, lax.rem(jnp.maximum(codes, 0), per_space))
    from_lane = lax.broadcasted_iota(jnp.int32, (LANES, LANES), 0)
    to_lane = lax.broadcasted_iota(jnp.int32, (LANES, LANES), 1)
    numbers = list(range(len(edges)))
    same = staged(numbers, edges, from_lane) == staged(numbers, edges, to_lane)
    upper = jnp.where(same, jnp.where(from_lane <= to_lane, 1.0, 0.0), 0.0).astype(BF16)
    same = jnp.where(same, 1.0, 0.0).astype(BF16)
    lower = lax.broadcasted_iota(jnp.int32, (owners, owners), 0) > lax.broadcasted_iota(jnp.int32, (owners, owners), 1)
    lower = jnp.where(lower, 1.0, 0.0).astype(BF16)
    row_lane = lax.broadcasted_iota(jnp.int32, (1, LANES), 1)
    location = jnp.zeros_like(codes)
    target = jnp.full_like(codes, -1)
    overflow = jnp.zeros((1, LANES), F32)
    for s in range(spaces):
        match = owner_of == s
        ones = jnp.where(match, 1.0, 0.0).astype(BF16)
        prefix = jnp.dot(ones, upper, preferred_element_type=F32)
        sums = jnp.dot(ones, same, preferred_element_type=F32)
        ahead = jnp.dot(lower, sums.astype(BF16), preferred_element_type=F32)
        totals = ahead[owners - 1:] + sums[owners - 1:]
        bases, running = [], jnp.zeros((1, LANES), F32)
        for edge, first, limit in zip(edges, (0,) + edges[:-1], limits):
            bases.append(running)
            running = running + jnp.broadcast_to(totals[:, first:first + 1], (1, LANES))
            overflow = jnp.maximum(overflow, jnp.where(running > limit, 1.0, 0.0))
        base = staged(bases, edges, row_lane)
        rank = (prefix + ahead + base).astype(jnp.int32) - 1
        d = lax.rem(here - s + spaces, spaces)
        places, begin = [], 0
        for limit in limits:
            places.append(spaces * begin + d * (limit - begin) + rank - begin)
            begin = limit
        location = jnp.where(match, staged(places, limits, rank), location)
        target = jnp.where(match, rank + s * pitch, target)
    local_ref[...] = pair_words(location)

    rows = spaces * pitch // LANES
    row_id = lax.broadcasted_iota(jnp.int32, (rows, LANES), 0)
    lane_of = (target & (LANES - 1)).astype(F32)
    lane_of = jnp.concatenate([lane_of, jnp.zeros((LANES - owners, LANES), F32)], axis=0).T
    high = jnp.zeros((rows, LANES), F32)
    low = jnp.zeros((rows, LANES), F32)
    for r in range(owners):
        hit = jnp.broadcast_to(target[r:r + 1] >> 7, (rows, LANES)) == row_id
        value = jnp.broadcast_to(within[r:r + 1], (rows, LANES))
        upper_part = jnp.where(hit, lax.shift_right_logical(value, 6), 0).astype(F32).astype(BF16)
        lower_part = jnp.where(hit, value & 63, 0).astype(F32).astype(BF16)
        column = jnp.broadcast_to(lane_of[:, r:r + 1], (LANES, LANES)).astype(jnp.int32)
        onehot = jnp.where(column == to_lane, 1.0, 0.0).astype(BF16)
        high += jnp.dot(upper_part, onehot, preferred_element_type=F32)
        low += jnp.dot(lower_part, onehot, preferred_element_type=F32)
    wanted = high.astype(jnp.int32) * 64 + low.astype(jnp.int32)
    words = pair_words(wanted)
    each = pitch // LANES
    for s in range(spaces):
        request_ref[s, 0:each, :] = words[s * each:(s + 1) * each]
        request_ref[s, each:, :] = jnp.broadcast_to(overflow.astype(jnp.int32), (ROWS - each, LANES))


def route(here, codes, spaces, per_space, limits, edges, interpret=False):
    return pl.pallas_call(
        functools.partial(route_kernel, limits, edges, per_space),
        out_shape=(
            jax.ShapeDtypeStruct((spaces, ROWS, LANES), jnp.int32),
            jax.ShapeDtypeStruct(codes.shape, jnp.int32),
        ),
        in_specs=[pl.BlockSpec(memory_space=pltpu.SMEM), pl.BlockSpec(memory_space=pltpu.VMEM)],
        out_specs=(pl.BlockSpec(memory_space=pltpu.VMEM), pl.BlockSpec(memory_space=pltpu.VMEM)),
        name="route",
        interpret=interpret,
    )(here, codes)


def lane_masks():
    low = lax.broadcasted_iota(jnp.int32, (ROWS, LANES), 1) < TILE
    return low, jnp.where(low, 1 << 24, 1 << 25)


def joined(a, b, word, low, bit):
    swap = (jnp.broadcast_to(word, (ROWS, LANES)) & bit) != 0
    crossed = jnp.where(low, b, a)
    crossed = jnp.concatenate([crossed[:, TILE:], crossed[:, :TILE]], axis=1)
    return jnp.where(swap, crossed, jnp.where(low, a, b))


def both(word):
    return word & 0xFFF, lax.shift_right_logical(word, 12) & 0xFFF


def pick_kernel(first_tile, words_ref, *refs):
    out_ref, source_ref, sems = refs[-3:]
    inputs = refs[:-3]
    step_owners, tiles = out_ref.shape[:2]
    start = pl.program_id(0) * step_owners * LANES
    low, bit = lane_masks()

    @pl.when(pl.program_id(0) == 0)
    def _():
        copies, begin = [], 0
        for p, part in enumerate(inputs):
            size = part.shape[0]
            copies.append(pltpu.make_async_copy(part, source_ref.at[pl.ds(begin, size)], sems.at[p]))
            begin += size
        for copy in copies:
            copy.start()
        for copy in copies:
            copy.wait()

    def owner(row, carry):
        def tile(k, carry):
            word = words_ref[start + row * LANES + (first_tile + k) * MAXB]
            first, second = both(word)
            for h in range(2):
                out_ref[row, k, h] = joined(source_ref[first, h], source_ref[second, h], word, low, bit)
            return carry

        return lax.fori_loop(0, tiles, tile, carry, unroll=tiles if tiles <= 16 else 4)

    lax.fori_loop(0, step_owners, owner, 0)


def gather_kernel(pitch, spans, words_ref, input_ref, *refs):
    outs, (source_ref, sem) = refs[:-2], refs[-2:]
    spaces = len(outs) // len(spans)
    low, bit = lane_masks()
    copy = pltpu.make_async_copy(input_ref, source_ref, sem)
    copy.start()
    copy.wait()
    for n, out_ref in enumerate(outs):
        begin = (n % spaces) * pitch + spans[n // spaces][0]

        def tile(k, carry):
            word = words_ref[begin + k * MAXB]
            first, second = both(word)
            for h in range(2):
                out_ref[k, h] = joined(source_ref[h, first], source_ref[h, second], word, low, bit)
            return carry

        lax.fori_loop(0, out_ref.shape[0], tile, 0, unroll=4)


def gather(words, source, spaces, spans, interpret=False):
    shapes = [((end - begin) // MAXB, 2, ROWS, LANES) for begin, end in spans for _ in range(spaces)]
    outs = pl.pallas_call(
        functools.partial(gather_kernel, words.shape[0] // spaces, spans),
        out_shape=[jax.ShapeDtypeStruct(shape, BF16) for shape in shapes],
        grid_spec=pltpu.PrefetchScalarGridSpec(
            num_scalar_prefetch=1,
            grid=(1,),
            in_specs=[pl.BlockSpec(memory_space=pl.ANY)],
            out_specs=[pl.BlockSpec(shape, lambda i, words: (0, 0, 0, 0)) for shape in shapes],
            scratch_shapes=[pltpu.VMEM(source.shape, BF16), pltpu.SemaphoreType.DMA],
        ),
        compiler_params=pltpu.CompilerParams(vmem_limit_bytes=40 << 20),
        name="gather",
        interpret=interpret,
    )(words, source)
    return [outs[n * spaces:(n + 1) * spaces] for n in range(len(spans))]


def in_hbm(shape, dtype, interpret):
    return jax.ShapeDtypeStruct(shape, dtype) if interpret else pltpu.HBM(shape, dtype)


def pick(words, parts, owners, first_tile, tiles, interpret=False):
    step = min(4, owners)
    size = sum(part.shape[0] for part in parts)
    return pl.pallas_call(
        functools.partial(pick_kernel, first_tile),
        out_shape=in_hbm((owners, tiles, 2, ROWS, LANES), BF16, interpret),
        grid_spec=pltpu.PrefetchScalarGridSpec(
            num_scalar_prefetch=1,
            grid=(owners // step,),
            in_specs=[pl.BlockSpec(memory_space=pl.ANY)] * len(parts),
            out_specs=pl.BlockSpec((step, tiles, 2, ROWS, LANES), lambda i, words: (i, 0, 0, 0, 0)),
            scratch_shapes=[
                pltpu.VMEM((size, 2, ROWS, LANES), BF16),
                pltpu.SemaphoreType.DMA((len(parts),)),
            ],
        ),
        compiler_params=pltpu.CompilerParams(vmem_limit_bytes=48 << 20),
        name="pick",
        interpret=interpret,
    )(words, *parts)


def project_kernel(group, starts, counts_ref, *refs):
    arrived, (weights_ref, basis_ref, remapped_ref, rounded_ref, partial_ref) = refs[:-5], refs[-5:]
    step = pl.program_id(0)

    @pl.when(step == 0)
    def _():
        partial_ref[...] = jnp.zeros_like(partial_ref)

    def remap(picked_ref):
        low = lax.broadcasted_iota(jnp.int32, (TILE, PAIR), 1) < TILE
        pieces = []
        for k in range(group):
            full = counts_ref[step * group + k] > 1
            weights = jnp.where(jnp.logical_or(low, full), weights_ref[k].astype(F32), 0.0).astype(BF16)
            picked = picked_ref[:, k].reshape(-1, PAIR)
            pieces.append(
                lax.dot_general(weights, picked, (((1,), (1,)), ((), ())), preferred_element_type=F32)
            )
        remapped_ref[...] = jnp.concatenate(pieces, axis=0).astype(BF16)

    for picked_ref, begin, end in zip(arrived, starts, starts[1:] + (None,)):
        here = step >= begin if end is None else jnp.logical_and(step >= begin, step < end)
        pl.when(here)(functools.partial(remap, picked_ref))

    add = jnp.dot(remapped_ref[...].T, basis_ref[...], preferred_element_type=F32)
    partial_ref[...] += add.reshape(partial_ref.shape)

    @pl.when(step == pl.num_programs(0) - 1)
    def _():
        rounded_ref[...] = partial_ref[...].astype(BF16)


def project(counts, arrived, weights, basis, interpret=False):
    owners = arrived[0].shape[0]
    snaps = owners * 2 * ROWS
    tiles = weights.shape[0]
    cells, rank = basis.shape
    group = 4
    starts, begin = [], 0
    for part in arrived:
        starts.append(begin)
        begin += part.shape[1] // group

    def chunk(start, part):
        last = part.shape[1] // group - 1
        return pl.BlockSpec(
            (owners, group, 2, ROWS, PAIR),
            lambda i, counts: (0, jnp.clip(i - start, 0, last), 0, 0, 0),
        )

    return pl.pallas_call(
        functools.partial(project_kernel, group, tuple(starts)),
        out_shape=(
            in_hbm((cells, snaps), BF16, interpret),
            jax.ShapeDtypeStruct((owners, 2 * ROWS, rank), BF16),
        ),
        grid_spec=pltpu.PrefetchScalarGridSpec(
            num_scalar_prefetch=1,
            grid=(tiles // group,),
            in_specs=[chunk(start, part) for start, part in zip(starts, arrived)] + [
                pl.BlockSpec((group, TILE, PAIR), lambda i, counts: (i, 0, 0)),
                pl.BlockSpec((group * TILE, rank), lambda i, counts: (i, 0)),
            ],
            out_specs=(
                pl.BlockSpec((group * TILE, snaps), lambda i, counts: (i, 0)),
                pl.BlockSpec((owners, 2 * ROWS, rank), lambda i, counts: (0, 0, 0)),
            ),
            scratch_shapes=[pltpu.VMEM((owners, 2 * ROWS, rank), F32)],
        ),
        compiler_params=pltpu.CompilerParams(vmem_limit_bytes=40 << 20),
        name="project",
        interpret=interpret,
    )(counts, *arrived, weights, basis)


def rotate_kernel(scale, remapped_ref, coeffs_ref, basis_ref, variances_ref, out_ref):
    update = jnp.dot(remapped_ref[...], coeffs_ref[...], preferred_element_type=F32)
    out_ref[...] = (basis_ref[...].astype(F32) * variances_ref[...] + update * scale).astype(BF16)


def rotate(remapped, coeffs, basis, variances, interpret=False):
    cells, rank = basis.shape
    snaps = remapped.shape[1]
    rows = min(256, cells)
    resident = lambda i: (0, 0)
    return pl.pallas_call(
        functools.partial(rotate_kernel, 1.0 / math.sqrt(snaps)),
        out_shape=in_hbm((cells, rank), BF16, interpret),
        grid=(cells // rows,),
        in_specs=[
            pl.BlockSpec((rows, snaps), lambda i: (i, 0)),
            pl.BlockSpec((snaps, rank), resident),
            pl.BlockSpec((rows, rank), lambda i: (i, 0)),
            pl.BlockSpec((1, rank), resident),
        ],
        out_specs=pl.BlockSpec((rows, rank), lambda i: (i, 0)),
        compiler_params=pltpu.CompilerParams(vmem_limit_bytes=40 << 20),
        name="rotate",
        interpret=interpret,
    )(remapped, coeffs, basis, variances[None, :])


def exchange(array, axis):
    return lax.all_to_all(array, axis, split_axis=0, concat_axis=0, tiled=True)


def spread(array, axis):
    return exchange(jnp.broadcast_to(array, (lax.axis_size(axis),) + array.shape), axis)


def per_device(interpret, limits, shares, snapshots, block_lists, tile_counts, remap_weights, basis, variances):
    tiles = block_lists.shape[0]
    owners, spaces = lax.axis_size("tm"), lax.axis_size("space")
    cells, rank = basis.shape
    total = cells * owners * spaces
    own_ranks = rank // spaces
    here = lax.axis_index("space")
    per_space = snapshots.shape[1] // TILE

    used = lax.broadcasted_iota(jnp.int32, block_lists.shape, 1) < tile_counts[:, None]
    codes = jnp.where(used, block_lists, -1).reshape(1, tiles * MAXB)
    codes = jnp.pad(codes, ((0, 0), (0, LANES - tiles * MAXB)), constant_values=-1)
    codes = spread(codes, "tm").reshape(owners, LANES)
    edges = tuple(share * MAXB for share in shares)
    requests, local_words = route(here[None], codes, spaces, per_space, limits, edges, interpret)
    asked = exchange(requests, "space")
    each = -(-limits[-1] // LANES)
    around = lax.dynamic_slice_in_dim(jnp.concatenate([asked, asked], axis=0), here, spaces, 0)
    asked_words = around[:, :each].reshape(-1)
    overflow = jnp.max(asked[:, each]) > 0
    chunks = [(begin, end - begin) for begin, end in zip((0,) + shares, shares)]

    def finish(arrived):
        remapped, partial = project(tile_counts, arrived, remap_weights, basis, interpret)
        parts = exchange(partial, "tm")
        column = spread(jnp.sum(parts.astype(F32), axis=0), "space")
        coeffs = jnp.sum(column, axis=0) * (1.0 / math.sqrt(total))
        half = coeffs.astype(BF16)
        rest = lax.dynamic_slice_in_dim(coeffs - half.astype(F32), here * own_ranks, own_ranks, 1)
        everyone = spread(jnp.concatenate([half, rest.astype(BF16)], axis=1), "tm")
        high = lax.dynamic_slice_in_dim(everyone, here * own_ranks, own_ranks, 2)
        own = high.astype(F32) + everyone[:, :, rank:].astype(F32)
        own_coeffs = own.reshape(owners * 2 * ROWS, own_ranks).T
        whole = everyone[:, :, :rank].reshape(owners * 2 * ROWS, rank)
        return own_coeffs, rotate(remapped, whole, basis, variances, interpret)

    def dense():
        words = pair_words_plain(jnp.maximum(codes, 0)).reshape(-1)
        local = snapshots.reshape(2, ROWS, -1, LANES).transpose(2, 0, 1, 3)
        source = spread(local, "space").reshape(-1, 2, ROWS, LANES)
        arrived = exchange(pick(words, [source], owners, 0, tiles, interpret), "tm")
        return finish([arrived[:, begin:begin + count] for begin, count in chunks])

    def sparse():
        local = snapshots.reshape(2, ROWS, -1, LANES).transpose(0, 2, 1, 3)
        spans = list(zip((0,) + limits, limits))
        sent = gather(asked_words, local, spaces, spans[:1], interpret)
        sent += gather(asked_words, local, spaces, spans[1:], interpret)
        words = local_words.reshape(-1)
        came, arrived = [], []
        for i, parts in enumerate(sent):
            came.append(parts[0])
            for d in range(1, spaces):
                ring = [(j, (j + d) % spaces) for j in range(spaces)]
                came.append(lax.ppermute(parts[d], "space", ring))
            chosen = pick(words, list(came), owners, *chunks[i], interpret)
            arrived.append(exchange(chosen, "tm"))
        return finish(arrived)

    return lax.cond(overflow, dense, sparse)


def pair_words_plain(index):
    after = jnp.roll(index, -1, axis=1)
    return (index >> 1) | ((after >> 1) << 12) | ((index & 1) << 24) | ((1 - (after & 1)) << 25)


def solution(mesh, interpret=False, limits=LIMITS, shares=SHARES):
    return jax.shard_map(
        functools.partial(per_device, interpret, limits, shares),
        mesh=mesh,
        in_specs=(
            P("tm", "space"),
            P(("tm", "space"), None),
            P(("tm", "space")),
            P(("tm", "space"), None, None),
            P(("tm", "space"), None),
            P(),
        ),
        out_specs=(P("space", None), P(("tm", "space"), None)),
        check_vma=False,
    )
```

```python
import functools
import math

import jax
import jax.numpy as jnp
from jax import lax
from jax.experimental import pallas as pl
from jax.experimental.pallas import tpu as pltpu
from jax.sharding import PartitionSpec as P


TILE = 64
MAXB = 2
PAIR = MAXB * TILE
ROWS = 8
LANES = 128
LIMITS = (112, 172, 256)
SHARES = (12, 20, 32)
BF16 = jnp.bfloat16
F32 = jnp.float32


def pair_words(index):
    after = pltpu.roll(index, LANES - 1, 1)
    return (
        lax.shift_right_logical(index, 1)
        | (lax.shift_right_logical(after, 1) << 12)
        | ((index & 1) << 24)
        | ((1 - (after & 1)) << 25)
    )


def staged(values, edges, at):
    result = values[-1]
    for value, edge in reversed(list(zip(values[:-1], edges[:-1]))):
        result = jnp.where(at < edge, value, result)
    return result


def route_kernel(limits, edges, per_space, here_ref, codes_ref, request_ref, local_ref):
    owners = codes_ref.shape[0]
    spaces = request_ref.shape[0]
    pitch = -(-limits[-1] // LANES) * LANES
    here = here_ref[0]
    codes = codes_ref[...]
    owner_of = jnp.where(codes < 0, -1, lax.div(jnp.maximum(codes, 0), per_space))
    within = jnp.where(codes < 0, 0, lax.rem(jnp.maximum(codes, 0), per_space))
    from_lane = lax.broadcasted_iota(jnp.int32, (LANES, LANES), 0)
    to_lane = lax.broadcasted_iota(jnp.int32, (LANES, LANES), 1)
    numbers = list(range(len(edges)))
    same = staged(numbers, edges, from_lane) == staged(numbers, edges, to_lane)
    upper = jnp.where(same, jnp.where(from_lane <= to_lane, 1.0, 0.0), 0.0).astype(BF16)
    same = jnp.where(same, 1.0, 0.0).astype(BF16)
    lower = lax.broadcasted_iota(jnp.int32, (owners, owners), 0) > lax.broadcasted_iota(jnp.int32, (owners, owners), 1)
    lower = jnp.where(lower, 1.0, 0.0).astype(BF16)
    row_lane = lax.broadcasted_iota(jnp.int32, (1, LANES), 1)
    location = jnp.zeros_like(codes)
    target = jnp.full_like(codes, -1)
    overflow = jnp.zeros((1, LANES), F32)
    for s in range(spaces):
        match = owner_of == s
        ones = jnp.where(match, 1.0, 0.0).astype(BF16)
        prefix = jnp.dot(ones, upper, preferred_element_type=F32)
        sums = jnp.dot(ones, same, preferred_element_type=F32)
        ahead = jnp.dot(lower, sums.astype(BF16), preferred_element_type=F32)
        totals = ahead[owners - 1:] + sums[owners - 1:]
        bases, running = [], jnp.zeros((1, LANES), F32)
        for edge, first, limit in zip(edges, (0,) + edges[:-1], limits):
            bases.append(running)
            running = running + jnp.broadcast_to(totals[:, first:first + 1], (1, LANES))
            overflow = jnp.maximum(overflow, jnp.where(running > limit, 1.0, 0.0))
        base = staged(bases, edges, row_lane)
        rank = (prefix + ahead + base).astype(jnp.int32) - 1
        d = lax.rem(here - s + spaces, spaces)
        places, begin = [], 0
        for limit in limits:
            places.append(spaces * begin + d * (limit - begin) + rank - begin)
            begin = limit
        location = jnp.where(match, staged(places, limits, rank), location)
        target = jnp.where(match, rank + s * pitch, target)
    local_ref[...] = pair_words(location)

    rows = spaces * pitch // LANES
    row_id = lax.broadcasted_iota(jnp.int32, (rows, LANES), 0)
    lane_of = (target & (LANES - 1)).astype(F32)
    lane_of = jnp.concatenate([lane_of, jnp.zeros((LANES - owners, LANES), F32)], axis=0).T
    high = jnp.zeros((rows, LANES), F32)
    low = jnp.zeros((rows, LANES), F32)
    for r in range(owners):
        hit = jnp.broadcast_to(target[r:r + 1] >> 7, (rows, LANES)) == row_id
        value = jnp.broadcast_to(within[r:r + 1], (rows, LANES))
        upper_part = jnp.where(hit, lax.shift_right_logical(value, 6), 0).astype(F32).astype(BF16)
        lower_part = jnp.where(hit, value & 63, 0).astype(F32).astype(BF16)
        column = jnp.broadcast_to(lane_of[:, r:r + 1], (LANES, LANES)).astype(jnp.int32)
        onehot = jnp.where(column == to_lane, 1.0, 0.0).astype(BF16)
        high += jnp.dot(upper_part, onehot, preferred_element_type=F32)
        low += jnp.dot(lower_part, onehot, preferred_element_type=F32)
    wanted = high.astype(jnp.int32) * 64 + low.astype(jnp.int32)
    words = pair_words(wanted)
    each = pitch // LANES
    for s in range(spaces):
        request_ref[s, 0:each, :] = words[s * each:(s + 1) * each]
        request_ref[s, each:, :] = jnp.broadcast_to(overflow.astype(jnp.int32), (ROWS - each, LANES))


def route(here, codes, spaces, per_space, limits, edges, interpret=False):
    return pl.pallas_call(
        functools.partial(route_kernel, limits, edges, per_space),
        out_shape=(
            jax.ShapeDtypeStruct((spaces, ROWS, LANES), jnp.int32),
            jax.ShapeDtypeStruct(codes.shape, jnp.int32),
        ),
        in_specs=[pl.BlockSpec(memory_space=pltpu.SMEM), pl.BlockSpec(memory_space=pltpu.VMEM)],
        out_specs=(pl.BlockSpec(memory_space=pltpu.VMEM), pl.BlockSpec(memory_space=pltpu.VMEM)),
        name="route",
        interpret=interpret,
    )(here, codes)


def lane_masks():
    low = lax.broadcasted_iota(jnp.int32, (ROWS, LANES), 1) < TILE
    return low, jnp.where(low, 1 << 24, 1 << 25)


def joined(a, b, word, low, bit):
    swap = (jnp.broadcast_to(word, (ROWS, LANES)) & bit) != 0
    crossed = jnp.where(low, b, a)
    crossed = jnp.concatenate([crossed[:, TILE:], crossed[:, :TILE]], axis=1)
    return jnp.where(swap, crossed, jnp.where(low, a, b))


def both(word):
    return word & 0xFFF, lax.shift_right_logical(word, 12) & 0xFFF


def pick_kernel(first_tile, words_ref, *refs):
    out_ref, source_ref, sems = refs[-3:]
    inputs = refs[:-3]
    step_owners, tiles = out_ref.shape[:2]
    start = pl.program_id(0) * step_owners * LANES
    low, bit = lane_masks()

    @pl.when(pl.program_id(0) == 0)
    def _():
        copies, begin = [], 0
        for p, part in enumerate(inputs):
            size = part.shape[0]
            copies.append(pltpu.make_async_copy(part, source_ref.at[pl.ds(begin, size)], sems.at[p]))
            begin += size
        for copy in copies:
            copy.start()
        for copy in copies:
            copy.wait()

    def owner(row, carry):
        def tile(k, carry):
            word = words_ref[start + row * LANES + (first_tile + k) * MAXB]
            first, second = both(word)
            for h in range(2):
                out_ref[row, k, h] = joined(source_ref[first, h], source_ref[second, h], word, low, bit)
            return carry

        return lax.fori_loop(0, tiles, tile, carry, unroll=tiles if tiles <= 16 else 4)

    lax.fori_loop(0, step_owners, owner, 0, unroll=2)


def gather_kernel(pitch, spans, words_ref, input_ref, *refs):
    outs, (source_ref, sem) = refs[:-2], refs[-2:]
    spaces = len(outs) // len(spans)
    low, bit = lane_masks()
    copy = pltpu.make_async_copy(input_ref, source_ref, sem)
    copy.start()
    copy.wait()
    for n, out_ref in enumerate(outs):
        begin = (n % spaces) * pitch + spans[n // spaces][0]

        def tile(k, carry):
            word = words_ref[begin + k * MAXB]
            first, second = both(word)
            for h in range(2):
                out_ref[k, h] = joined(source_ref[h, first], source_ref[h, second], word, low, bit)
            return carry

        count = out_ref.shape[0]
        lax.fori_loop(0, count, tile, 0, unroll=max(u for u in range(1, 15) if count % u == 0))


def gather(words, source, spaces, spans, interpret=False):
    shapes = [((end - begin) // MAXB, 2, ROWS, LANES) for begin, end in spans for _ in range(spaces)]
    outs = pl.pallas_call(
        functools.partial(gather_kernel, words.shape[0] // spaces, spans),
        out_shape=[in_hbm(shape, BF16, interpret) for shape in shapes],
        grid_spec=pltpu.PrefetchScalarGridSpec(
            num_scalar_prefetch=1,
            grid=(1,),
            in_specs=[pl.BlockSpec(memory_space=pl.ANY)],
            out_specs=[pl.BlockSpec(shape, lambda i, words: (0, 0, 0, 0)) for shape in shapes],
            scratch_shapes=[pltpu.VMEM(source.shape, BF16), pltpu.SemaphoreType.DMA],
        ),
        compiler_params=pltpu.CompilerParams(vmem_limit_bytes=40 << 20),
        name="gather",
        interpret=interpret,
    )(words, source)
    return [outs[n * spaces:(n + 1) * spaces] for n in range(len(spans))]


def in_hbm(shape, dtype, interpret):
    return jax.ShapeDtypeStruct(shape, dtype) if interpret else pltpu.HBM(shape, dtype)


def pick(words, parts, owners, first_tile, tiles, interpret=False):
    step = min(4, owners)
    size = sum(part.shape[0] for part in parts)
    return pl.pallas_call(
        functools.partial(pick_kernel, first_tile),
        out_shape=in_hbm((owners, tiles, 2, ROWS, LANES), BF16, interpret),
        grid_spec=pltpu.PrefetchScalarGridSpec(
            num_scalar_prefetch=1,
            grid=(owners // step,),
            in_specs=[pl.BlockSpec(memory_space=pl.ANY if interpret else pltpu.HBM)] * len(parts),
            out_specs=pl.BlockSpec((step, tiles, 2, ROWS, LANES), lambda i, words: (i, 0, 0, 0, 0)),
            scratch_shapes=[
                pltpu.VMEM((size, 2, ROWS, LANES), BF16),
                pltpu.SemaphoreType.DMA((len(parts),)),
            ],
        ),
        compiler_params=pltpu.CompilerParams(vmem_limit_bytes=48 << 20),
        name="pick",
        interpret=interpret,
    )(words, *parts)


def project_kernel(group, starts, counts_ref, *refs):
    arrived, (weights_ref, basis_ref, remapped_ref, rounded_ref, partial_ref) = refs[:-5], refs[-5:]
    step = pl.program_id(0)

    @pl.when(step == 0)
    def _():
        partial_ref[...] = jnp.zeros_like(partial_ref)

    def remap(picked_ref):
        low = lax.broadcasted_iota(jnp.int32, (TILE, PAIR), 1) < TILE
        pieces = []
        for k in range(group):
            full = counts_ref[step * group + k] > 1
            weights = jnp.where(jnp.logical_or(low, full), weights_ref[k].astype(F32), 0.0).astype(BF16)
            picked = picked_ref[:, k].reshape(-1, PAIR)
            pieces.append(
                lax.dot_general(weights, picked, (((1,), (1,)), ((), ())), preferred_element_type=F32)
            )
        remapped_ref[...] = jnp.concatenate(pieces, axis=0).astype(BF16)

    for picked_ref, begin, end in zip(arrived, starts, starts[1:] + (None,)):
        here = step >= begin if end is None else jnp.logical_and(step >= begin, step < end)
        pl.when(here)(functools.partial(remap, picked_ref))

    add = jnp.dot(remapped_ref[...].T, basis_ref[...], preferred_element_type=F32)
    partial_ref[...] += add.reshape(partial_ref.shape)

    @pl.when(step == pl.num_programs(0) - 1)
    def _():
        rounded_ref[...] = partial_ref[...].astype(BF16)


def project(counts, arrived, weights, basis, interpret=False):
    owners = arrived[0].shape[0]
    snaps = owners * 2 * ROWS
    tiles = weights.shape[0]
    cells, rank = basis.shape
    group = 4
    starts, begin = [], 0
    for part in arrived:
        starts.append(begin)
        begin += part.shape[1] // group

    def chunk(start, part):
        last = part.shape[1] // group - 1
        return pl.BlockSpec(
            (owners, group, 2, ROWS, PAIR),
            lambda i, counts: (0, jnp.clip(i - start, 0, last), 0, 0, 0),
        )

    return pl.pallas_call(
        functools.partial(project_kernel, group, tuple(starts)),
        out_shape=(
            in_hbm((cells, snaps), BF16, interpret),
            jax.ShapeDtypeStruct((owners, 2 * ROWS, rank), BF16),
        ),
        grid_spec=pltpu.PrefetchScalarGridSpec(
            num_scalar_prefetch=1,
            grid=(tiles // group,),
            in_specs=[chunk(start, part) for start, part in zip(starts, arrived)] + [
                pl.BlockSpec((group, TILE, PAIR), lambda i, counts: (i, 0, 0)),
                pl.BlockSpec((group * TILE, rank), lambda i, counts: (i, 0)),
            ],
            out_specs=(
                pl.BlockSpec((group * TILE, snaps), lambda i, counts: (i, 0)),
                pl.BlockSpec((owners, 2 * ROWS, rank), lambda i, counts: (0, 0, 0)),
            ),
            scratch_shapes=[pltpu.VMEM((owners, 2 * ROWS, rank), F32)],
        ),
        compiler_params=pltpu.CompilerParams(vmem_limit_bytes=40 << 20),
        name="project",
        interpret=interpret,
    )(counts, *arrived, weights, basis)


def rotate_kernel(scale, remapped_ref, coeffs_ref, basis_ref, variances_ref, out_ref):
    update = jnp.dot(remapped_ref[...], coeffs_ref[...], preferred_element_type=F32)
    out_ref[...] = (basis_ref[...].astype(F32) * variances_ref[...] + update * scale).astype(BF16)


def rotate(remapped, coeffs, basis, variances, interpret=False):
    cells, rank = basis.shape
    snaps = remapped.shape[1]
    rows = min(256, cells)
    resident = lambda i: (0, 0)
    return pl.pallas_call(
        functools.partial(rotate_kernel, 1.0 / math.sqrt(snaps)),
        out_shape=in_hbm((cells, rank), BF16, interpret),
        grid=(cells // rows,),
        in_specs=[
            pl.BlockSpec((rows, snaps), lambda i: (i, 0)),
            pl.BlockSpec((snaps, rank), resident),
            pl.BlockSpec((rows, rank), lambda i: (i, 0)),
            pl.BlockSpec((1, rank), resident),
        ],
        out_specs=pl.BlockSpec((rows, rank), lambda i: (i, 0)),
        compiler_params=pltpu.CompilerParams(vmem_limit_bytes=40 << 20),
        name="rotate",
        interpret=interpret,
    )(remapped, coeffs, basis, variances[None, :])


def exchange(array, axis):
    return lax.all_to_all(array, axis, split_axis=0, concat_axis=0, tiled=True)


def spread(array, axis):
    return exchange(jnp.broadcast_to(array, (lax.axis_size(axis),) + array.shape), axis)


def per_device(interpret, limits, shares, snapshots, block_lists, tile_counts, remap_weights, basis, variances):
    tiles = block_lists.shape[0]
    owners, spaces = lax.axis_size("tm"), lax.axis_size("space")
    cells, rank = basis.shape
    total = cells * owners * spaces
    own_ranks = rank // spaces
    here = lax.axis_index("space")
    per_space = snapshots.shape[1] // TILE

    used = lax.broadcasted_iota(jnp.int32, block_lists.shape, 1) < tile_counts[:, None]
    codes = jnp.where(used, block_lists, -1).reshape(1, tiles * MAXB)
    codes = jnp.pad(codes, ((0, 0), (0, LANES - tiles * MAXB)), constant_values=-1)
    codes = spread(codes, "tm").reshape(owners, LANES)
    edges = tuple(share * MAXB for share in shares)
    requests, local_words = route(here[None], codes, spaces, per_space, limits, edges, interpret)
    asked = exchange(requests, "space")
    each = -(-limits[-1] // LANES)
    around = lax.dynamic_slice_in_dim(jnp.concatenate([asked, asked], axis=0), here, spaces, 0)
    asked_words = around[:, :each].reshape(-1)
    overflow = jnp.max(asked[:, each]) > 0
    chunks = [(begin, end - begin) for begin, end in zip((0,) + shares, shares)]

    def finish(arrived):
        remapped, partial = project(tile_counts, arrived, remap_weights, basis, interpret)
        parts = exchange(partial, "tm")
        column = spread(jnp.sum(parts.astype(F32), axis=0), "space")
        coeffs = jnp.sum(column, axis=0) * (1.0 / math.sqrt(total))
        half = coeffs.astype(BF16)
        rest = lax.dynamic_slice_in_dim(coeffs - half.astype(F32), here * own_ranks, own_ranks, 1)
        everyone = spread(jnp.concatenate([half, rest.astype(BF16)], axis=1), "tm")
        high = lax.dynamic_slice_in_dim(everyone, here * own_ranks, own_ranks, 2)
        own = high.astype(F32) + everyone[:, :, rank:].astype(F32)
        own_coeffs = own.reshape(owners * 2 * ROWS, own_ranks).T
        whole = everyone[:, :, :rank].reshape(owners * 2 * ROWS, rank)
        return own_coeffs, rotate(remapped, whole, basis, variances, interpret)

    def dense():
        words = pair_words_plain(jnp.maximum(codes, 0)).reshape(-1)
        local = snapshots.reshape(2, ROWS, -1, LANES).transpose(2, 0, 1, 3)
        source = spread(local, "space").reshape(-1, 2, ROWS, LANES)
        arrived = exchange(pick(words, [source], owners, 0, tiles, interpret), "tm")
        return finish([arrived[:, begin:begin + count] for begin, count in chunks])

    def sparse():
        local = snapshots.reshape(2, ROWS, -1, LANES).transpose(0, 2, 1, 3)
        spans = list(zip((0,) + limits, limits))
        sent = gather(asked_words, local, spaces, spans[:1], interpret)
        sent += gather(asked_words, local, spaces, spans[1:], interpret)
        words = local_words.reshape(-1)
        came, arrived = [], []
        for i, parts in enumerate(sent):
            came.append(parts[0])
            for d in range(1, spaces):
                ring = [(j, (j + d) % spaces) for j in range(spaces)]
                came.append(lax.ppermute(parts[d], "space", ring))
            parts = came if interpret else [
                pltpu.with_memory_space_constraint(part, pltpu.HBM) for part in came
            ]
            chosen = pick(words, list(parts), owners, *chunks[i], interpret)
            arrived.append(exchange(chosen, "tm"))
        return finish(arrived)

    return lax.cond(overflow, dense, sparse)


def pair_words_plain(index):
    after = jnp.roll(index, -1, axis=1)
    return (index >> 1) | ((after >> 1) << 12) | ((index & 1) << 24) | ((1 - (after & 1)) << 25)


def solution(mesh, interpret=False, limits=LIMITS, shares=SHARES):
    return jax.shard_map(
        functools.partial(per_device, interpret, limits, shares),
        mesh=mesh,
        in_specs=(
            P("tm", "space"),
            P(("tm", "space"), None),
            P(("tm", "space")),
            P(("tm", "space"), None, None),
            P(("tm", "space"), None),
            P(),
        ),
        out_specs=(P("space", None), P(("tm", "space"), None)),
        check_vma=False,
    )
```
